32 devices in a mesh: sweep: 2 (over x), na: 16 (over z, y, core).
Axes of the slice: x: 2, y: 2, z: 4, core: 2. Of those that a mesh axis runs over, the one named last changes fastest.
Arguments:
- hierarchy: float32 [32, 16, 2, 128, 128], P(('sweep', 'na')), parts along dimension 0, may hold values from -6 to 6
- hamiltonian: float32 [128, 128], replicated, may hold values from -0.5 to 0.5
- couplings: float32 [2, 128, 128], replicated, may hold values from -0.5 to 0.5
- damp_rates: float32 [4], P('sweep'), parts along dimension 0, may hold values from 0.5 to 2
- coef_real: float32 [4], P('sweep'), parts along dimension 0, may hold values from 0.5 to 2
- coef_imag: float32 [4], P('sweep'), parts along dimension 0, may hold values from -1 to 1
Outputs:
- evolved: float32 [32, 16, 2, 128, 128], P(('sweep', 'na')), parts along dimension 0
The draws below stay inside these ranges and needn't reach their ends.
There are 2 independent parts, one for each index of `sweep`. The reference program is written for one: setup_inputs(seed, part) draws one part's arguments, and reference() takes and returns one part's arrays. A program takes and returns all parts, laid end to end along the dimension named above; an argument that names none is the same for every part. Nothing has to cross between parts.
All inputs are finite; a program needn't handle non-finite values.
Results may differ from the reference program's by a relative error of at most 0.0001.
Values sent between devices are 32-bit elements; how exact they have to be, the bound alone decides.
A program may use at most 128 MiB of HBM per device.

```python
import math
import jax
import jax.numpy as jnp
from jax import lax

M = 128
STEPS = 1
N_NA = 16


def shard_levels(own_key, dims, shards, least, top_value):
    factor_of, own = 1.0, jax.random.fold_in(own_key, 6)
    for dim, parts in shards:
        heights = jnp.exp(jax.random.uniform(jax.random.fold_in(own, dim), (parts,), jnp.float32, least / len(shards), top_value / len(shards)))
        factor_of = factor_of * jnp.repeat(heights, dims[dim] // parts).reshape([-1 if axis == dim else 1 for axis in range(len(dims))])
    return factor_of


def normal_values(key, dims, width, most, shards=(), held_as=jnp.bfloat16):
    gain = shard_levels(key, dims, shards, -0.22, 0.18) if shards else 1.0
    drawn = jax.random.normal(key, dims, jnp.float32) * width * gain
    return jnp.minimum(jnp.maximum(drawn, -most), most).astype(held_as)


def setup_inputs(seed: int = 0, part: int = 0) -> dict:
    splits = jax.random.split(jax.random.key(seed), 7)
    part_splits = jax.random.split(jax.random.fold_in(splits[6], part), 7)
    hierarchy = normal_values(part_splits[0], (N_NA, N_NA, 2, M, M), 1.0, 6.0, ((0, 16),), jnp.float32)
    hamiltonian = normal_values(splits[1], (M, M), M ** -0.5, 0.5, (), jnp.float32)
    couplings = normal_values(splits[2], (2, M, M), M ** -0.5, 0.5, (), jnp.float32)
    damp_rates = jnp.clip(jnp.exp(jax.random.uniform(part_splits[3], (2,), jnp.float32, math.log(0.5), math.log(2.0))), 0.5, 2.0)
    coef_real = jnp.clip(jnp.exp(jax.random.uniform(part_splits[4], (2,), jnp.float32, math.log(0.5), math.log(2.0))), 0.5, 2.0)
    coef_imag = jnp.clip(jax.random.uniform(part_splits[5], (2,), jnp.float32, -1.0, 1.0), -1.0, 1.0)
    return dict(hierarchy=hierarchy, hamiltonian=hamiltonian, couplings=couplings, damp_rates=damp_rates, coef_real=coef_real, coef_imag=coef_imag)


step_size = 0.02

def evolve(values, raise_one, lower_one, raise_two, lower_two, first_mode, second_mode, alive_mask, hamilton, coupled, damp_rates, coef_real, coef_imag):
    matrix_order = values.shape[-1]
    magnitude = jnp.sqrt(coef_real * coef_real + coef_imag * coef_imag)
    left_terms = [values]
    right_terms = [values]
    mode_terms = ((raise_one, lower_one, first_mode), (raise_two, lower_two, second_mode))
    for which_mode in range(2):
        raised, lowered, occupied = mode_terms[which_mode]
        raise_weight = jnp.sqrt((occupied + 1.0) * magnitude[which_mode])[..., None, None]
        lower_weight = jnp.sqrt(occupied / magnitude[which_mode])[..., None, None]
        real_coef = coef_real[which_mode]
        imag_coef = coef_imag[which_mode]
        shared_re = raise_weight * raised[..., 0, :, :]
        shared_im = raise_weight * raised[..., 1, :, :]
        direct_re = lower_weight * (real_coef * lowered[..., 0, :, :])
        direct_im = lower_weight * (real_coef * lowered[..., 1, :, :])
        cross_re = lower_weight * (imag_coef * lowered[..., 1, :, :])
        cross_im = lower_weight * (imag_coef * lowered[..., 0, :, :])
        left_terms.append(jnp.stack([shared_re + direct_re - cross_re, shared_im + direct_im + cross_im], axis=-3))
        right_terms.append(jnp.stack([shared_re + direct_re + cross_re, shared_im + direct_im - cross_im], axis=-3))
    operators = (hamilton, coupled[0], coupled[1])
    flat_shape = (-1, 2, matrix_order, matrix_order)
    left_sum = sum((jnp.einsum('ab,scbd->scad', operand, stacked.reshape(flat_shape), precision=lax.Precision.HIGHEST) for operand, stacked in zip(operators, left_terms)))
    right_sum = sum((jnp.einsum('scab,bd->scad', stacked.reshape(flat_shape), operand, precision=lax.Precision.HIGHEST) for operand, stacked in zip(operators, right_terms)))
    damping = (first_mode * damp_rates[0] + second_mode * damp_rates[1]).reshape((-1, 1, 1))
    flat_values = values.reshape(flat_shape)
    change_re = left_sum[:, 1] - right_sum[:, 1] - damping * flat_values[:, 0]
    change_im = right_sum[:, 0] - left_sum[:, 0] - damping * flat_values[:, 1]
    change = jnp.stack([change_re, change_im], axis=1).reshape(values.shape)
    return change * alive_mask[..., None, None, None]

def reference(hierarchy, hamiltonian, couplings, damp_rates, coef_real, coef_imag):
    total_slots = hierarchy.shape[0]
    hamilton = 0.5 * (hamiltonian + hamiltonian.T)
    coupled = 0.5 * (couplings + jnp.swapaxes(couplings, 1, 2))
    slot_index = jnp.arange(total_slots)
    first_mode = jnp.broadcast_to(slot_index[:, None], (total_slots, total_slots)).astype(jnp.float32)
    second_mode = jnp.broadcast_to(slot_index[None, :], (total_slots, total_slots)).astype(jnp.float32)
    alive_mask = (first_mode + second_mode <= total_slots - 1).astype(jnp.float32)

    def derivative(values):
        pad_first = jnp.zeros_like(values[:1])
        pad_second = jnp.zeros_like(values[:, :1])
        raise_one = jnp.concatenate([values[1:], pad_first], 0)
        lower_one = jnp.concatenate([pad_first, values[:-1]], 0)
        raise_two = jnp.concatenate([values[:, 1:], pad_second], 1)
        lower_two = jnp.concatenate([pad_second, values[:, :-1]], 1)
        return evolve(values, raise_one, lower_one, raise_two, lower_two, first_mode, second_mode, alive_mask, hamilton, coupled, damp_rates, coef_real, coef_imag)
    values = hierarchy * alive_mask[..., None, None, None]
    for step_index in range(STEPS):
        middle = values + 0.5 * step_size * derivative(values)
        values = values + step_size * derivative(middle)
    return values
```

```python
import functools
import jax
import jax.numpy as jnp
from jax import lax
from jax.experimental import pallas as pl
from jax.experimental.pallas import tpu as pltpu
from jax.sharding import PartitionSpec as P

step_size = 0.02
MESH = pl.DeviceIdType.MESH
NEAR, OWN, PARTNER, FAR = 0, 1, 2, 3
STRIP = 32
LAG = 2
EARLY = 3


def split(x):
    high = x.astype(jnp.bfloat16)
    return high, (x - high.astype(jnp.float32)).astype(jnp.bfloat16)


def kernel(
    total,
    order,
    hier_ref,
    ham_ref,
    coup_ref,
    damp_in,
    creal_in,
    cimag_in,
    out_ref,
    rho,
    mid,
    w_left,
    w_right,
    x_left,
    x_right,
    table,
    ham_buf,
    damp_ref,
    creal_ref,
    cimag_ref,
    own_sem,
    ham_sem,
    small_sem,
    send_sem,
    recv_sem,
):
    M, N = order, total
    p = lax.axis_index("na")
    chip = p // 2
    core = p % 2
    odd = chip % 2
    chips = N // 2
    first = core == 0
    K = N - p
    pairs = N - 1 - 2 * chip

    is_relay = core != odd
    relays = jnp.logical_and(
        is_relay, jnp.where(odd == 1, chip >= 2, chip + 2 < chips)
    )
    fed_by_relay = jnp.logical_and(
        core == odd, jnp.where(odd == 1, chip + 2 < chips, chip >= 2)
    )
    direct_to = jnp.where(odd == 1, 2 * chip - 1, 2 * chip + 2)
    relay_to = jnp.where(odd == 1, p - 3, p + 3)
    relay_from = jnp.where(odd == 1, p + 3, p - 3)

    direct_count = jnp.where(p == 0, K - 2, K)
    near_count = jnp.where(first, jnp.where(p == 0, 0, K + 1), K - 1)
    far_count = jnp.where(
        first,
        jnp.where(
            p == 0, 0, jnp.where(jnp.logical_and(odd == 1, chip >= 2), K + 2, K)
        ),
        jnp.maximum(K - 2, 0),
    )
    relay_near_count = jnp.where(relays, jnp.where(first, near_count, K - 3), 0)
    relay_far_count = jnp.where(relays, far_count, 0)
    mid_near_count = jnp.where(first, jnp.where(p == 0, 0, K), K - 1)
    direct_slot = jnp.where(core == odd, FAR, NEAR)

    def own_copy(i):
        return pltpu.make_async_copy(
            hier_ref.at[0, i], rho.at[OWN, i], own_sem.at[i]
        )

    def operator_copy(k):
        return pltpu.make_async_copy(
            ham_ref if k == 0 else coup_ref.at[k - 1], ham_buf.at[k], ham_sem.at[k]
        )

    def remote(src, dst, send, recv, i, target):
        return pltpu.make_async_remote_copy(
            src_ref=src,
            dst_ref=dst,
            send_sem=send_sem.at[send, i],
            recv_sem=recv_sem.at[recv, i],
            device_id={"na": target},
            device_id_type=MESH,
        )

    def direct_copy(i):
        return remote(
            hier_ref.at[0, i], rho.at[direct_slot, i], 0, direct_slot, i, direct_to
        )

    def partner_copy(i):
        return remote(
            hier_ref.at[0, i], rho.at[PARTNER, i], 1, PARTNER, i, p + 1 - 2 * core
        )

    def relay_near(i):
        return remote(rho.at[NEAR, i], rho.at[FAR, i], 2, FAR, i, relay_to)

    def relay_far(i):
        return remote(rho.at[FAR, i], rho.at[NEAR, i], 3, NEAR, i, relay_to)

    def mid_copy(i):
        return remote(
            mid.at[OWN, i], mid.at[PARTNER, i], 4, 1, i, p + 1 - 2 * core
        )

    def arrival(which, i):
        return remote(
            rho.at[which, i], rho.at[which, i], 0, which, i, p + 1 - 2 * core
        )

    barrier = pltpu.get_barrier_semaphore()

    def greet(target):
        pl.semaphore_signal(
            barrier, inc=1, device_id={"na": target}, device_id_type=MESH
        )

    greet(p + 1 - 2 * core)
    greet(direct_to)

    @pl.when(is_relay)
    def _():
        greet(jnp.where(odd == 1, p - 2, p + 2))

    @pl.when(relays)
    def _():
        greet(relay_to)

    @pl.when(fed_by_relay)
    def _():
        greet(relay_from)

    pl.semaphore_wait(
        barrier,
        2
        + is_relay.astype(jnp.int32)
        + relays.astype(jnp.int32)
        + fed_by_relay.astype(jnp.int32),
    )

    @pl.loop(0, K)
    def _(i):
        @pl.when(i < direct_count)
        def _():
            direct_copy(i).start()

        @pl.when(i < pairs)
        def _():
            partner_copy(i).start()

    small = [
        pltpu.make_async_copy(source, target, small_sem.at[k])
        for k, (source, target) in enumerate(
            ((damp_in, damp_ref), (creal_in, creal_ref), (cimag_in, cimag_ref))
        )
    ]
    for k in range(3):
        small[k].start()
        operator_copy(k).start()

    @pl.loop(0, K)
    def _(i):
        own_copy(i).start()

    for k in range(3):
        operator_copy(k).wait()
        raw = ham_buf[k]
        high, low = split(0.5 * (raw + raw.T))
        for half in range(2):
            cols = slice((3 * half + k) * M, (3 * half + k + 1) * M)
            w_left[0:M, cols] = high
            w_left[M : 2 * M, cols] = low
            w_right[cols, 0:M] = high
            w_right[cols, M : 2 * M] = low

    for copy in small:
        copy.wait()

    for mode in range(2):
        re = jnp.full((8, M), creal_ref[mode], jnp.float32)
        im = jnp.full((8, M), cimag_ref[mode], jnp.float32)
        magnitude = jnp.sqrt(re * re + im * im)

        @pl.loop(0, N)
        def _(n):
            occupied = jnp.full((8, M), n.astype(jnp.float32), jnp.float32)
            lower = jnp.sqrt(occupied / magnitude)
            table[3 * mode, n] = jnp.sqrt((occupied + 1.0) * magnitude)
            table[3 * mode + 1, n] = lower * re
            table[3 * mode + 2, n] = lower * im

    @pl.loop(K, N)
    def _(i):
        out_ref[0, i] = jnp.zeros((2, M, M), jnp.float32)

    def derivative(buf, own, up, down, q, n, base, scale, store):
        alive = q + n < N - 1
        alive_scale = jnp.where(alive, 1.0, 0.0)
        up = jnp.where(alive, up, own)
        above = jnp.where(alive, n + 1, n)
        below = jnp.maximum(n - 1, 0)
        terms = []
        for mode, occupied in ((0, q), (1, n)):
            terms.append(
                (
                    table[3 * mode, occupied, 0:1, :] * alive_scale,
                    table[3 * mode + 1, occupied, 0:1, :],
                    table[3 * mode + 2, occupied, 0:1, :],
                )
            )
        sources = (((up, n), (down, n)), ((own, above), (own, below)))

        def put(block, rows, part, left, right):
            for x, is_left in ((left, True), (right, False)):
                high, low = split(x)
                for half, value in ((0, high), (1, low)):
                    at = (3 * half + block) * M
                    if is_left:
                        x_left[
                            at + rows : at + rows + STRIP, part * M : (part + 1) * M
                        ] = value
                    else:
                        x_right[
                            part * M + rows : part * M + rows + STRIP, at : at + M
                        ] = value

        for rows in range(0, M, STRIP):
            strip = slice(rows, rows + STRIP)
            for part in range(2):
                high, low = split(buf[own, n, part, strip, :])
                for half, value in ((0, high), (1, low)):
                    at = 3 * half * M
                    x_left[
                        at + rows : at + rows + STRIP, part * M : (part + 1) * M
                    ] = value
                    x_right[
                        part * M + rows : part * M + rows + STRIP, at : at + M
                    ] = value
            for mode in range(2):
                raise_w, direct_w, cross_w = terms[mode]
                (ub, us), (vb, vs) = sources[mode]
                v_re = buf[vb, vs, 0, strip, :]
                v_im = buf[vb, vs, 1, strip, :]
                e_re = raise_w * buf[ub, us, 0, strip, :] + direct_w * v_re
                e_im = raise_w * buf[ub, us, 1, strip, :] + direct_w * v_im
                x_re = cross_w * v_im
                x_im = cross_w * v_re
                put(1 + mode, rows, 0, e_re - x_re, e_re + x_re)
                put(1 + mode, rows, 1, e_im + x_im, e_im - x_im)
        left = jnp.dot(w_left[...], x_left[...], preferred_element_type=jnp.float32)
        right = jnp.dot(x_right[...], w_right[...], preferred_element_type=jnp.float32)
        damping = q.astype(jnp.float32) * damp_ref[0] + n.astype(jnp.float32) * damp_ref[1]
        left = left[0:M] + left[M : 2 * M]
        right = right[:, 0:M] + right[:, M : 2 * M]
        change_re = left[:, M : 2 * M] - right[M : 2 * M] - damping * buf[own, n, 0]
        change_im = right[0:M] - left[:, 0:M] - damping * buf[own, n, 1]
        store(0, base(0) + scale * change_re)
        store(1, base(1) + scale * change_im)

    up = jnp.where(first, PARTNER, NEAR)
    down = jnp.where(first, jnp.where(p == 0, OWN, NEAR), PARTNER)
    near_up = jnp.where(first, OWN, FAR)
    near_down = jnp.where(first, FAR, OWN)
    near_q = jnp.where(first, p - 1, p + 1)

    def take(i):
        @pl.when(i < near_count)
        def _():
            arrival(NEAR, i).wait_recv()

        @pl.when(i < relay_near_count)
        def _():
            relay_near(i).start()

        @pl.when(i < far_count)
        def _():
            arrival(FAR, i).wait_recv()

        @pl.when(i < relay_far_count)
        def _():
            relay_far(i).start()

    def middle(which, i, up, down, q):
        def store(part, value):
            mid[which, i, part] = value

        derivative(
            rho, which, up, down, q, i,
            lambda part: rho[which, i, part], 0.5 * step_size, store,
        )

    early = jnp.logical_and(core == 1, K - 1 > EARLY + 1)
    in_turn = jnp.where(early, K - 1, K)

    @pl.loop(0, K)
    def _(i):
        own_copy(i).wait()

    lag = jnp.where(jnp.logical_or(p == 1, p == 2), 1, LAG)

    @pl.loop(-1, K + lag)
    def _(i):
        j = i - lag

        @pl.when(j >= 0)
        def _():
            @pl.when(j < pairs)
            def _():
                mid_copy(j).wait_recv()

            def store(part, value):
                out_ref[0, j, part] = value

            derivative(
                mid, OWN, up, down, p, j,
                lambda part: rho[OWN, j, part], step_size, store,
            )

        take(i + 1)

        @pl.when(jnp.logical_and(i < EARLY, i + 1 < pairs))
        def _():
            arrival(PARTNER, i + 1).wait_recv()

        @pl.when(i == EARLY)
        def _():
            @pl.loop(EARLY + 1, pairs)
            def _(k):
                arrival(PARTNER, k).wait_recv()

        @pl.when(i + 1 < in_turn)
        def _():
            middle(OWN, i + 1, up, down, p)

        @pl.when(jnp.logical_and(early, i == EARLY))
        def _():
            middle(OWN, K - 1, up, down, p)

        @pl.when(jnp.logical_and(i >= 0, i < mid_near_count))
        def _():
            middle(NEAR, i, near_up, near_down, near_q)

        @pl.when(jnp.logical_and(i + 1 < pairs, i + 1 < in_turn))
        def _():
            mid_copy(i + 1).start()

        @pl.when(jnp.logical_and(early, i == EARLY))
        def _():
            mid_copy(K - 1).start()

    @pl.loop(0, N)
    def _(i):
        @pl.when(i < direct_count)
        def _():
            direct_copy(i).wait_send()

        @pl.when(i < pairs)
        def _():
            partner_copy(i).wait_send()
            mid_copy(i).wait_send()

        @pl.when(i < relay_near_count)
        def _():
            relay_near(i).wait_send()

        @pl.when(i < relay_far_count)
        def _():
            relay_far(i).wait_send()


def per_device(hierarchy, hamiltonian, couplings, damp_rates, coef_real, coef_imag):
    total = hierarchy.shape[1]
    M = hierarchy.shape[-1]
    hbm = pl.BlockSpec(memory_space=pltpu.HBM)
    return pl.pallas_call(
        functools.partial(kernel, total, M),
        out_shape=pltpu.VMEM(hierarchy.shape, jnp.float32),
        in_specs=[hbm] * 6,
        out_specs=pl.BlockSpec(memory_space=pltpu.VMEM),
        scratch_shapes=[
            pltpu.VMEM((4, total, 2, M, M), jnp.float32),
            pltpu.VMEM((3, total, 2, M, M), jnp.float32),
            pltpu.VMEM((2 * M, 6 * M), jnp.bfloat16),
            pltpu.VMEM((6 * M, 2 * M), jnp.bfloat16),
            pltpu.VMEM((6 * M, 2 * M), jnp.bfloat16),
            pltpu.VMEM((2 * M, 6 * M), jnp.bfloat16),
            pltpu.VMEM((6, total, 8, M), jnp.float32),
            pltpu.VMEM((3, M, M), jnp.float32),
            pltpu.SMEM(damp_rates.shape, jnp.float32),
            pltpu.SMEM(coef_real.shape, jnp.float32),
            pltpu.SMEM(coef_imag.shape, jnp.float32),
            pltpu.SemaphoreType.DMA((total,)),
            pltpu.SemaphoreType.DMA((3,)),
            pltpu.SemaphoreType.DMA((3,)),
            pltpu.SemaphoreType.DMA((5, total)),
            pltpu.SemaphoreType.DMA((4, total)),
        ],
        compiler_params=pltpu.CompilerParams(
            collective_id=0, has_side_effects=True, vmem_limit_bytes=(8 + total) * 2**20
        ),
    )(
        *(
            pltpu.with_memory_space_constraint(x, pltpu.HBM)
            for x in (
                hierarchy,
                hamiltonian,
                couplings,
                damp_rates,
                coef_real,
                coef_imag,
            )
        )
    )


def solution(mesh):
    in_specs = (
        P(("sweep", "na"), None, None, None, None),
        P(),
        P(),
        P("sweep"),
        P("sweep"),
        P("sweep"),
    )
    out_specs = P(("sweep", "na"), None, None, None, None)
    return jax.shard_map(
        per_device, mesh=mesh, in_specs=in_specs, out_specs=out_specs, check_vma=False
    )
```

```python
import functools
import jax
import jax.numpy as jnp
from jax import lax
from jax.experimental import pallas as pl
from jax.experimental.pallas import tpu as pltpu
from jax.sharding import PartitionSpec as P

step_size = 0.02
MESH = pl.DeviceIdType.MESH
NEAR, OWN, PARTNER, FAR = 0, 1, 2, 3
STRIP = 32
LAG = 2
EARLY = 3


def split(x):
    high = x.astype(jnp.bfloat16)
    return high, (x - high.astype(jnp.float32)).astype(jnp.bfloat16)


def kernel(
    total,
    order,
    hier_ref,
    ham_ref,
    coup_ref,
    damp_in,
    creal_in,
    cimag_in,
    out_ref,
    rho,
    mid,
    w_left,
    w_right,
    x_left,
    x_right,
    table,
    ham_buf,
    damp_ref,
    creal_ref,
    cimag_ref,
    own_sem,
    ham_sem,
    small_sem,
    send_sem,
    recv_sem,
):
    M, N = order, total
    p = lax.axis_index("na")
    chip = p // 2
    core = p % 2
    odd = chip % 2
    chips = N // 2
    first = core == 0
    K = N - p
    pairs = N - 1 - 2 * chip

    is_relay = core != odd
    relays = jnp.logical_and(
        is_relay, jnp.where(odd == 1, chip >= 2, chip + 2 < chips)
    )
    fed_by_relay = jnp.logical_and(
        core == odd, jnp.where(odd == 1, chip + 2 < chips, chip >= 2)
    )
    direct_to = jnp.where(odd == 1, 2 * chip - 1, 2 * chip + 2)
    relay_to = jnp.where(odd == 1, p - 3, p + 3)
    relay_from = jnp.where(odd == 1, p + 3, p - 3)

    direct_count = jnp.where(p == 0, K - 2, K)
    near_count = jnp.where(first, jnp.where(p == 0, 0, K + 1), K - 1)
    far_count = jnp.where(
        first,
        jnp.where(
            p == 0, 0, jnp.where(jnp.logical_and(odd == 1, chip >= 2), K + 2, K)
        ),
        jnp.maximum(K - 2, 0),
    )
    relay_near_count = jnp.where(relays, jnp.where(first, near_count, K - 3), 0)
    relay_far_count = jnp.where(relays, far_count, 0)
    mid_near_count = jnp.where(first, jnp.where(p == 0, 0, K), K - 1)
    direct_slot = jnp.where(core == odd, FAR, NEAR)

    def own_copy(i):
        return pltpu.make_async_copy(
            hier_ref.at[0, i], rho.at[OWN, i], own_sem.at[i]
        )

    def operator_copy(k):
        return pltpu.make_async_copy(
            ham_ref if k == 0 else coup_ref.at[k - 1], ham_buf.at[k], ham_sem.at[k]
        )

    def remote(src, dst, send, recv, i, target):
        return pltpu.make_async_remote_copy(
            src_ref=src,
            dst_ref=dst,
            send_sem=send_sem.at[send, i],
            recv_sem=recv_sem.at[recv, i],
            device_id={"na": target},
            device_id_type=MESH,
        )

    def direct_copy(i):
        return remote(
            hier_ref.at[0, i], rho.at[direct_slot, i], 0, direct_slot, i, direct_to
        )

    def partner_copy(i):
        return remote(
            hier_ref.at[0, i], rho.at[PARTNER, i], 1, PARTNER, i, p + 1 - 2 * core
        )

    def relay_near(i):
        return remote(rho.at[NEAR, i], rho.at[FAR, i], 2, FAR, i, relay_to)

    def relay_far(i):
        return remote(rho.at[FAR, i], rho.at[NEAR, i], 3, NEAR, i, relay_to)

    def mid_copy(i):
        return remote(
            mid.at[OWN, i], mid.at[PARTNER, i], 4, 1, i, p + 1 - 2 * core
        )

    def arrival(which, i):
        return remote(
            rho.at[which, i], rho.at[which, i], 0, which, i, p + 1 - 2 * core
        )

    barrier = pltpu.get_barrier_semaphore()

    def greet(target):
        pl.semaphore_signal(
            barrier, inc=1, device_id={"na": target}, device_id_type=MESH
        )

    greet(p + 1 - 2 * core)
    greet(direct_to)

    @pl.when(is_relay)
    def _():
        greet(jnp.where(odd == 1, p - 2, p + 2))

    @pl.when(relays)
    def _():
        greet(relay_to)

    @pl.when(fed_by_relay)
    def _():
        greet(relay_from)

    pl.semaphore_wait(
        barrier,
        2
        + is_relay.astype(jnp.int32)
        + relays.astype(jnp.int32)
        + fed_by_relay.astype(jnp.int32),
    )

    @pl.loop(0, K)
    def _(i):
        @pl.when(i < direct_count)
        def _():
            direct_copy(i).start()

        @pl.when(i < pairs)
        def _():
            partner_copy(i).start()

    small = [
        pltpu.make_async_copy(source, target, small_sem.at[k])
        for k, (source, target) in enumerate(
            ((damp_in, damp_ref), (creal_in, creal_ref), (cimag_in, cimag_ref))
        )
    ]
    for k in range(3):
        small[k].start()
        operator_copy(k).start()

    @pl.loop(0, K)
    def _(i):
        own_copy(i).start()

    for k in range(3):
        operator_copy(k).wait()
        raw = ham_buf[k]
        high, low = split(0.5 * (raw + raw.T))
        for half in range(2):
            cols = slice((3 * half + k) * M, (3 * half + k + 1) * M)
            w_left[0:M, cols] = high
            w_left[M : 2 * M, cols] = low
            w_right[cols, 0:M] = high
            w_right[cols, M : 2 * M] = low

    for copy in small:
        copy.wait()

    for mode in range(2):
        re = jnp.full((8, M), creal_ref[mode], jnp.float32)
        im = jnp.full((8, M), cimag_ref[mode], jnp.float32)
        magnitude = jnp.sqrt(re * re + im * im)

        @pl.loop(0, N)
        def _(n):
            occupied = jnp.full((8, M), n.astype(jnp.float32), jnp.float32)
            lower = jnp.sqrt(occupied / magnitude)
            table[3 * mode, n] = jnp.sqrt((occupied + 1.0) * magnitude)
            table[3 * mode + 1, n] = lower * re
            table[3 * mode + 2, n] = lower * im

    @pl.loop(K, N)
    def _(i):
        out_ref[0, i] = jnp.zeros((2, M, M), jnp.float32)

    def neighbours(own, up, down, q, n):
        alive = q + n < N - 1
        alive_scale = jnp.where(alive, 1.0, 0.0)
        up = jnp.where(alive, up, own)
        above = jnp.where(alive, n + 1, n)
        below = jnp.maximum(n - 1, 0)
        modes = []
        for mode, occupied, raised, lowered in (
            (0, q, (up, n), (down, n)),
            (1, n, (own, above), (own, below)),
        ):
            modes.append(
                (
                    table[3 * mode, occupied, 0:1, :] * alive_scale,
                    table[3 * mode + 1, occupied, 0:1, :],
                    table[3 * mode + 2, occupied, 0:1, :],
                    raised,
                    lowered,
                )
            )
        return modes

    def build(task, buf, own, n, modes):
        def put(block, rows, part, x, is_left):
            high, low = split(x)
            across = (2 * task + part) * M
            for half, value in ((0, high), (1, low)):
                at = (3 * half + block) * M
                if is_left:
                    x_left[at + rows : at + rows + STRIP, across : across + M] = value
                else:
                    x_right[across + rows : across + rows + STRIP, at : at + M] = value

        for rows in range(0, M, STRIP):
            strip = slice(rows, rows + STRIP)
            for part in range(2):
                value = buf[own, n, part, strip, :]
                put(0, rows, part, value, True)
                put(0, rows, part, value, False)
            for mode in range(2):
                raise_w, direct_w, cross_w, (ub, us), (vb, vs) = modes[mode]
                v_re = buf[vb, vs, 0, strip, :]
                v_im = buf[vb, vs, 1, strip, :]
                e_re = raise_w * buf[ub, us, 0, strip, :] + direct_w * v_re
                e_im = raise_w * buf[ub, us, 1, strip, :] + direct_w * v_im
                x_re = cross_w * v_im
                x_im = cross_w * v_re
                put(1 + mode, rows, 0, e_re - x_re, True)
                put(1 + mode, rows, 0, e_re + x_re, False)
                put(1 + mode, rows, 1, e_im + x_im, True)
                put(1 + mode, rows, 1, e_im - x_im, False)

    def advance(buf, scale, tasks):
        count = len(tasks)
        for task, (own, up, down, q, n, base, store) in enumerate(tasks):
            build(task, buf, own, n, neighbours(own, up, down, q, n))
        wide = 2 * M * count
        lefts = jnp.dot(
            w_left[...], x_left[:, 0:wide], preferred_element_type=jnp.float32
        )
        rights = jnp.dot(
            x_right[0:wide, :], w_right[...], preferred_element_type=jnp.float32
        )
        for task, (own, up, down, q, n, base, store) in enumerate(tasks):
            damping = (
                q.astype(jnp.float32) * damp_ref[0] + n.astype(jnp.float32) * damp_ref[1]
            )
            across = slice(2 * M * task, 2 * M * (task + 1))
            left = lefts[0:M, across] + lefts[M : 2 * M, across]
            right = rights[across, 0:M] + rights[across, M : 2 * M]
            change_re = left[:, M : 2 * M] - right[M : 2 * M] - damping * buf[own, n, 0]
            change_im = right[0:M] - left[:, 0:M] - damping * buf[own, n, 1]
            store(0, base(0) + scale * change_re)
            store(1, base(1) + scale * change_im)

    up = jnp.where(first, PARTNER, NEAR)
    down = jnp.where(first, jnp.where(p == 0, OWN, NEAR), PARTNER)
    near_up = jnp.where(first, OWN, FAR)
    near_down = jnp.where(first, FAR, OWN)
    near_q = jnp.where(first, p - 1, p + 1)

    def take(i):
        @pl.when(i < near_count)
        def _():
            arrival(NEAR, i).wait_recv()

        @pl.when(i < relay_near_count)
        def _():
            relay_near(i).start()

        @pl.when(i < far_count)
        def _():
            arrival(FAR, i).wait_recv()

        @pl.when(i < relay_far_count)
        def _():
            relay_far(i).start()

    def middle(which, i, up, down, q):
        def store(part, value):
            mid[which, i, part] = value

        return (which, up, down, q, i, lambda part: rho[which, i, part], store)

    def own_middle(i):
        return middle(OWN, i, up, down, p)

    def near_middle(i):
        return middle(NEAR, i, near_up, near_down, near_q)

    def final(j):
        def store(part, value):
            out_ref[0, j, part] = value

        return (OWN, up, down, p, j, lambda part: rho[OWN, j, part], store)

    early = jnp.logical_and(core == 1, K - 1 > EARLY + 1)
    in_turn = jnp.where(early, K - 1, K)

    @pl.loop(0, K)
    def _(i):
        own_copy(i).wait()

    lag = jnp.where(jnp.logical_or(p == 1, p == 2), 1, LAG)

    @pl.loop(-1, K + lag)
    def _(i):
        j = i - lag

        @pl.when(j >= 0)
        def _():
            @pl.when(j < pairs)
            def _():
                mid_copy(j).wait_recv()

            advance(mid, step_size, [final(j)])

        take(i + 1)

        @pl.when(jnp.logical_and(i < EARLY, i + 1 < pairs))
        def _():
            arrival(PARTNER, i + 1).wait_recv()

        @pl.when(i == EARLY)
        def _():
            @pl.loop(EARLY + 1, pairs)
            def _(k):
                arrival(PARTNER, k).wait_recv()

        own_now = i + 1 < in_turn
        near_now = jnp.logical_and(i >= 0, i < mid_near_count)
        both = jnp.logical_and(own_now, near_now)
        ahead = jnp.logical_and(early, i == EARLY)

        @pl.when(both)
        def _():
            advance(rho, 0.5 * step_size, [own_middle(i + 1), near_middle(i)])

        @pl.when(jnp.logical_or(own_now != both, ahead))
        def _():
            advance(rho, 0.5 * step_size, [own_middle(jnp.where(both, K - 1, i + 1))])

        @pl.when(near_now != both)
        def _():
            advance(rho, 0.5 * step_size, [near_middle(i)])

        @pl.when(jnp.logical_and(i + 1 < pairs, i + 1 < in_turn))
        def _():
            mid_copy(i + 1).start()

        @pl.when(jnp.logical_and(early, i == EARLY))
        def _():
            mid_copy(K - 1).start()

    @pl.loop(0, N)
    def _(i):
        @pl.when(i < direct_count)
        def _():
            direct_copy(i).wait_send()

        @pl.when(i < pairs)
        def _():
            partner_copy(i).wait_send()
            mid_copy(i).wait_send()

        @pl.when(i < relay_near_count)
        def _():
            relay_near(i).wait_send()

        @pl.when(i < relay_far_count)
        def _():
            relay_far(i).wait_send()


def per_device(hierarchy, hamiltonian, couplings, damp_rates, coef_real, coef_imag):
    total = hierarchy.shape[1]
    M = hierarchy.shape[-1]
    hbm = pl.BlockSpec(memory_space=pltpu.HBM)
    return pl.pallas_call(
        functools.partial(kernel, total, M),
        out_shape=pltpu.VMEM(hierarchy.shape, jnp.float32),
        in_specs=[hbm] * 6,
        out_specs=pl.BlockSpec(memory_space=pltpu.VMEM),
        scratch_shapes=[
            pltpu.VMEM((4, total, 2, M, M), jnp.float32),
            pltpu.VMEM((3, total, 2, M, M), jnp.float32),
            pltpu.VMEM((2 * M, 6 * M), jnp.bfloat16),
            pltpu.VMEM((6 * M, 2 * M), jnp.bfloat16),
            pltpu.VMEM((6 * M, 4 * M), jnp.bfloat16),
            pltpu.VMEM((4 * M, 6 * M), jnp.bfloat16),
            pltpu.VMEM((6, total, 8, M), jnp.float32),
            pltpu.VMEM((3, M, M), jnp.float32),
            pltpu.SMEM(damp_rates.shape, jnp.float32),
            pltpu.SMEM(coef_real.shape, jnp.float32),
            pltpu.SMEM(coef_imag.shape, jnp.float32),
            pltpu.SemaphoreType.DMA((total,)),
            pltpu.SemaphoreType.DMA((3,)),
            pltpu.SemaphoreType.DMA((3,)),
            pltpu.SemaphoreType.DMA((5, total)),
            pltpu.SemaphoreType.DMA((4, total)),
        ],
        compiler_params=pltpu.CompilerParams(
            collective_id=0, has_side_effects=True, vmem_limit_bytes=(8 + total) * 2**20
        ),
    )(
        *(
            pltpu.with_memory_space_constraint(x, pltpu.HBM)
            for x in (
                hierarchy,
                hamiltonian,
                couplings,
                damp_rates,
                coef_real,
                coef_imag,
            )
        )
    )


def solution(mesh):
    in_specs = (
        P(("sweep", "na"), None, None, None, None),
        P(),
        P(),
        P("sweep"),
        P("sweep"),
        P("sweep"),
    )
    out_specs = P(("sweep", "na"), None, None, None, None)
    return jax.shard_map(
        per_device, mesh=mesh, in_specs=in_specs, out_specs=out_specs, check_vma=False
    )
```

```python
import functools
import jax
import jax.numpy as jnp
from jax import lax
from jax.experimental import pallas as pl
from jax.experimental.pallas import tpu as pltpu
from jax.sharding import PartitionSpec as P

step_size = 0.02
MESH = pl.DeviceIdType.MESH
NEAR, OWN, PARTNER, FAR, MID = 0, 1, 2, 3, 4
STRIP = 32
LAG = 2
EARLY = 3
LOW = (6, 4)
HIGH = (5, 3)
PASS_DOWN = 2
FINAL, MIDDLE, SIDE = 0, 1, 2


def split(x):
    high = x.astype(jnp.bfloat16)
    return high, (x - high.astype(jnp.float32)).astype(jnp.bfloat16)


def kernel(
    total,
    order,
    hier_ref,
    ham_ref,
    coup_ref,
    damp_in,
    creal_in,
    cimag_in,
    out_ref,
    rho,
    w_left,
    w_right,
    x_left,
    x_right,
    table,
    ham_buf,
    damp_ref,
    creal_ref,
    cimag_ref,
    own_sem,
    ham_sem,
    small_sem,
    send_sem,
    recv_sem,
):
    M, N = order, total
    p = lax.axis_index("na")
    chip = p // 2
    core = p % 2
    odd = chip % 2
    chips = N // 2
    first = core == 0
    K = N - p
    pairs = N - 1 - 2 * chip

    is_relay = core != odd
    relays = jnp.logical_and(
        is_relay, jnp.where(odd == 1, chip >= 2, chip + 2 < chips)
    )
    fed_by_relay = jnp.logical_and(
        core == odd, jnp.where(odd == 1, chip + 2 < chips, chip >= 2)
    )
    direct_to = jnp.where(odd == 1, 2 * chip - 1, 2 * chip + 2)
    relay_to = jnp.where(odd == 1, p - 3, p + 3)
    relay_from = jnp.where(odd == 1, p + 3, p - 3)

    direct_count = jnp.where(p == 0, K - 2, K)
    near_count = jnp.where(first, jnp.where(p == 0, 0, K + 1), K - 1)
    far_count = jnp.where(
        first,
        jnp.where(
            p == 0, 0, jnp.where(jnp.logical_and(odd == 1, chip >= 2), K + 2, K)
        ),
        jnp.maximum(K - 2, 0),
    )
    relay_near_count = jnp.where(relays, jnp.where(first, near_count, K - 3), 0)
    relay_far_count = jnp.where(relays, far_count, 0)
    mid_near_count = jnp.where(first, jnp.where(p == 0, 0, K), K - 1)
    direct_slot = jnp.where(core == odd, FAR, NEAR)

    def detour_low(i):
        return jnp.logical_and(i >= N - LOW[0], i < N - LOW[1])

    def detour_high(i):
        return jnp.logical_and(i >= N - HIGH[0], i < N - HIGH[1])

    def via_upper(i):
        return jnp.logical_or(
            jnp.logical_and(p == 2, detour_low(i)),
            jnp.logical_and(p == 3, detour_high(i)),
        )

    def direct_target(i):
        return jnp.where(via_upper(i), 4, direct_to)

    def waits_near(i):
        early = jnp.logical_and(p == 4, detour_high(i))
        return jnp.logical_and(i < near_count, jnp.logical_not(early))

    def waits_far(i):
        early = jnp.logical_and(p == 4, detour_low(i))
        return jnp.logical_and(i < far_count, jnp.logical_not(early))

    def passes_near(i):
        spared = jnp.logical_and(p == 1, detour_low(i))
        return jnp.logical_and(i < relay_near_count, jnp.logical_not(spared))

    def passes_far(i):
        spared = jnp.logical_and(p == 1, detour_high(i))
        return jnp.logical_and(i < relay_far_count, jnp.logical_not(spared))

    relay_to = jnp.where(p == 4, 1, relay_to)

    def own_copy(i):
        return pltpu.make_async_copy(
            hier_ref.at[0, i], rho.at[OWN, i], own_sem.at[i]
        )

    def operator_copy(k):
        return pltpu.make_async_copy(
            ham_ref if k == 0 else coup_ref.at[k - 1], ham_buf.at[k], ham_sem.at[k]
        )

    def remote(src, dst, send, recv, i, target):
        return pltpu.make_async_remote_copy(
            src_ref=src,
            dst_ref=dst,
            send_sem=send_sem.at[send, i],
            recv_sem=recv_sem.at[recv, i],
            device_id={"na": target},
            device_id_type=MESH,
        )

    def direct_copy(i):
        slot = jnp.where(via_upper(i), NEAR + FAR - direct_slot, direct_slot)
        return remote(
            hier_ref.at[0, i], rho.at[slot, i], 0, slot, i, direct_target(i)
        )

    def partner_copy(i):
        return remote(
            hier_ref.at[0, i], rho.at[PARTNER, i], 1, PARTNER, i, p + 1 - 2 * core
        )

    def relay_near(i):
        return remote(rho.at[NEAR, i], rho.at[FAR, i], 2, FAR, i, relay_to)

    def relay_far(i):
        return remote(rho.at[FAR, i], rho.at[NEAR, i], 3, NEAR, i, relay_to)

    def mid_copy(i):
        return remote(
            rho.at[MID + OWN, i], rho.at[MID + PARTNER, i], 4, 1, i, p + 1 - 2 * core
        )

    def arrival(which, i):
        return remote(
            rho.at[which, i], rho.at[which, i], 0, which, i, p + 1 - 2 * core
        )

    barrier = pltpu.get_barrier_semaphore()

    def greet(target):
        pl.semaphore_signal(
            barrier, inc=1, device_id={"na": target}, device_id_type=MESH
        )

    greet(p + 1 - 2 * core)
    greet(direct_to)

    @pl.when(is_relay)
    def _():
        greet(jnp.where(odd == 1, p - 2, p + 2))

    @pl.when(relays)
    def _():
        greet(relay_to)

    @pl.when(fed_by_relay)
    def _():
        greet(relay_from)

    for one, other in ((2, 4), (3, 4)):
        for me, peer in ((one, other), (other, one)):

            @pl.when(p == me)
            def _(peer=peer):
                greet(peer)

    pl.semaphore_wait(
        barrier,
        2
        + jnp.where(jnp.logical_or(p == 2, p == 3), 1, 0)
        + jnp.where(p == 4, 2, 0)
        + is_relay.astype(jnp.int32)
        + relays.astype(jnp.int32)
        + fed_by_relay.astype(jnp.int32),
    )

    @pl.loop(0, K)
    def _(i):
        @pl.when(i < direct_count)
        def _():
            direct_copy(i).start()

        @pl.when(i < pairs)
        def _():
            partner_copy(i).start()

    small = [
        pltpu.make_async_copy(source, target, small_sem.at[k])
        for k, (source, target) in enumerate(
            ((damp_in, damp_ref), (creal_in, creal_ref), (cimag_in, cimag_ref))
        )
    ]
    for k in range(3):
        small[k].start()
        operator_copy(k).start()

    @pl.loop(0, K)
    def _(i):
        own_copy(i).start()

    for k in range(3):
        operator_copy(k).wait()
        raw = ham_buf[k]
        high, low = split(0.5 * (raw + raw.T))
        for half in range(2):
            cols = slice((3 * half + k) * M, (3 * half + k + 1) * M)
            w_left[0:M, cols] = high
            w_left[M : 2 * M, cols] = low
            w_right[cols, 0:M] = high
            w_right[cols, M : 2 * M] = low

    for copy in small:
        copy.wait()

    for mode in range(2):
        re = jnp.full((8, M), creal_ref[mode], jnp.float32)
        im = jnp.full((8, M), cimag_ref[mode], jnp.float32)
        magnitude = jnp.sqrt(re * re + im * im)

        @pl.loop(0, N)
        def _(n):
            occupied = jnp.full((8, M), n.astype(jnp.float32), jnp.float32)
            lower = jnp.sqrt(occupied / magnitude)
            table[3 * mode, n] = jnp.sqrt((occupied + 1.0) * magnitude)
            table[3 * mode + 1, n] = lower * re
            table[3 * mode + 2, n] = lower * im

    @pl.loop(K, N)
    def _(i):
        out_ref[0, i] = jnp.zeros((2, M, M), jnp.float32)

    def advance(own, up, down, q, n, base, scale, store):
        alive = q + n < N - 1
        alive_scale = jnp.where(alive, 1.0, 0.0)
        up = jnp.where(alive, up, own)
        above = jnp.where(alive, n + 1, n)
        below = jnp.maximum(n - 1, 0)

        def put(block, rows, part, x, is_left):
            high, low = split(x)
            for half, value in ((0, high), (1, low)):
                at = (3 * half + block) * M
                if is_left:
                    x_left[
                        at + rows : at + rows + STRIP, part * M : (part + 1) * M
                    ] = value
                else:
                    x_right[
                        part * M + rows : part * M + rows + STRIP, at : at + M
                    ] = value

        for rows in range(0, M, STRIP):
            strip = slice(rows, rows + STRIP)
            for part in range(2):
                value = rho[own, n, part, strip, :]
                put(0, rows, part, value, True)
                put(0, rows, part, value, False)
            for mode, occupied, (ub, us), (vb, vs) in (
                (0, q, (up, n), (down, n)),
                (1, n, (own, above), (own, below)),
            ):
                raise_w = table[3 * mode, occupied, 0:1, :] * alive_scale
                direct_w = table[3 * mode + 1, occupied, 0:1, :]
                cross_w = table[3 * mode + 2, occupied, 0:1, :]
                v_re = rho[vb, vs, 0, strip, :]
                v_im = rho[vb, vs, 1, strip, :]
                e_re = raise_w * rho[ub, us, 0, strip, :] + direct_w * v_re
                e_im = raise_w * rho[ub, us, 1, strip, :] + direct_w * v_im
                x_re = cross_w * v_im
                x_im = cross_w * v_re
                put(1 + mode, rows, 0, e_re - x_re, True)
                put(1 + mode, rows, 0, e_re + x_re, False)
                put(1 + mode, rows, 1, e_im + x_im, True)
                put(1 + mode, rows, 1, e_im - x_im, False)
        left = jnp.dot(w_left[...], x_left[...], preferred_element_type=jnp.float32)
        right = jnp.dot(x_right[...], w_right[...], preferred_element_type=jnp.float32)
        damping = (
            q.astype(jnp.float32) * damp_ref[0] + n.astype(jnp.float32) * damp_ref[1]
        )
        left = left[0:M] + left[M : 2 * M]
        right = right[:, 0:M] + right[:, M : 2 * M]
        change_re = left[:, M : 2 * M] - right[M : 2 * M] - damping * rho[own, n, 0]
        change_im = right[0:M] - left[:, 0:M] - damping * rho[own, n, 1]
        store(rho[base, n, 0] + scale * change_re, rho[base, n, 1] + scale * change_im)

    up = jnp.where(first, PARTNER, NEAR)
    down = jnp.where(first, jnp.where(p == 0, OWN, NEAR), PARTNER)
    near_up = jnp.where(first, OWN, FAR)
    near_down = jnp.where(first, FAR, OWN)
    near_q = jnp.where(first, p - 1, p + 1)

    def take(i):
        @pl.when(waits_near(i))
        def _():
            arrival(NEAR, i).wait_recv()

        @pl.when(passes_near(i))
        def _():
            relay_near(i).start()

        @pl.when(waits_far(i))
        def _():
            arrival(FAR, i).wait_recv()

        @pl.when(passes_far(i))
        def _():
            relay_far(i).start()

    early = jnp.logical_and(core == 1, K - 1 > EARLY + 1)
    in_turn = jnp.where(early, K - 1, K)

    @pl.loop(0, K)
    def _(i):
        own_copy(i).wait()

    lag = jnp.where(jnp.logical_and(relays, p != 1), LAG, 1)

    @pl.loop(-1, K + lag)
    def _(i):
        j = i - lag
        ahead = jnp.logical_and(early, i == EARLY)

        @pl.loop(0, jnp.where(ahead, 4, 3))
        def _(kind):
            is_final = kind == FINAL
            is_near = kind == SIDE

            @pl.when(jnp.logical_and(is_final, jnp.logical_and(j >= 0, j < pairs)))
            def _():
                mid_copy(j).wait_recv()

            @pl.when(kind == MIDDLE)
            def _():
                @pl.when(jnp.logical_and(p == 4, i == PASS_DOWN))
                def _():
                    @pl.loop(N - LOW[0], N - LOW[1])
                    def _(k):
                        arrival(FAR, k).wait_recv()
                        relay_far(k).start()

                    @pl.loop(N - HIGH[0], N - HIGH[1])
                    def _(k):
                        arrival(NEAR, k).wait_recv()
                        relay_near(k).start()

                take(i + 1)

                @pl.when(jnp.logical_and(i < EARLY, i + 1 < pairs))
                def _():
                    arrival(PARTNER, i + 1).wait_recv()

                @pl.when(i == EARLY)
                def _():
                    @pl.loop(EARLY + 1, pairs)
                    def _(k):
                        arrival(PARTNER, k).wait_recv()

            n = jnp.where(
                is_final,
                j,
                jnp.where(is_near, i, jnp.where(kind == MIDDLE, i + 1, K - 1)),
            )
            limit = jnp.where(
                is_final,
                K,
                jnp.where(is_near, mid_near_count, jnp.where(kind == MIDDLE, in_turn, K)),
            )

            @pl.when(jnp.logical_and(n >= 0, n < limit))
            def _():
                shift = jnp.where(is_final, MID, 0)
                source = jnp.where(is_near, NEAR, OWN)

                def store(real, imag):
                    @pl.when(is_final)
                    def _():
                        out_ref[0, n, 0] = real
                        out_ref[0, n, 1] = imag

                    @pl.when(jnp.logical_not(is_final))
                    def _():
                        rho[MID + source, n, 0] = real
                        rho[MID + source, n, 1] = imag

                advance(
                    shift + source,
                    shift + jnp.where(is_near, near_up, up),
                    shift + jnp.where(is_near, near_down, down),
                    jnp.where(is_near, near_q, p),
                    n,
                    source,
                    jnp.where(is_final, step_size, 0.5 * step_size),
                    store,
                )

                @pl.when(
                    jnp.logical_and(jnp.logical_not(is_final | is_near), n < pairs)
                )
                def _():
                    mid_copy(n).start()

    @pl.loop(0, N)
    def _(i):
        @pl.when(i < direct_count)
        def _():
            direct_copy(i).wait_send()

        @pl.when(i < pairs)
        def _():
            partner_copy(i).wait_send()
            mid_copy(i).wait_send()

        @pl.when(
            jnp.logical_or(passes_near(i), jnp.logical_and(p == 4, detour_high(i)))
        )
        def _():
            relay_near(i).wait_send()

        @pl.when(jnp.logical_or(passes_far(i), jnp.logical_and(p == 4, detour_low(i))))
        def _():
            relay_far(i).wait_send()


def per_device(hierarchy, hamiltonian, couplings, damp_rates, coef_real, coef_imag):
    total = hierarchy.shape[1]
    M = hierarchy.shape[-1]
    hbm = pl.BlockSpec(memory_space=pltpu.HBM)
    return pl.pallas_call(
        functools.partial(kernel, total, M),
        out_shape=pltpu.VMEM(hierarchy.shape, jnp.float32),
        in_specs=[hbm] * 6,
        out_specs=pl.BlockSpec(memory_space=pltpu.VMEM),
        scratch_shapes=[
            pltpu.VMEM((MID + 3, total, 2, M, M), jnp.float32),
            pltpu.VMEM((2 * M, 6 * M), jnp.bfloat16),
            pltpu.VMEM((6 * M, 2 * M), jnp.bfloat16),
            pltpu.VMEM((6 * M, 2 * M), jnp.bfloat16),
            pltpu.VMEM((2 * M, 6 * M), jnp.bfloat16),
            pltpu.VMEM((6, total, 8, M), jnp.float32),
            pltpu.VMEM((3, M, M), jnp.float32),
            pltpu.SMEM(damp_rates.shape, jnp.float32),
            pltpu.SMEM(coef_real.shape, jnp.float32),
            pltpu.SMEM(coef_imag.shape, jnp.float32),
            pltpu.SemaphoreType.DMA((total,)),
            pltpu.SemaphoreType.DMA((3,)),
            pltpu.SemaphoreType.DMA((3,)),
            pltpu.SemaphoreType.DMA((5, total)),
            pltpu.SemaphoreType.DMA((4, total)),
        ],
        compiler_params=pltpu.CompilerParams(
            collective_id=0, has_side_effects=True, vmem_limit_bytes=(8 + total) * 2**20
        ),
    )(
        *(
            pltpu.with_memory_space_constraint(x, pltpu.HBM)
            for x in (
                hierarchy,
                hamiltonian,
                couplings,
                damp_rates,
                coef_real,
                coef_imag,
            )
        )
    )


def solution(mesh):
    in_specs = (
        P(("sweep", "na"), None, None, None, None),
        P(),
        P(),
        P("sweep"),
        P("sweep"),
        P("sweep"),
    )
    out_specs = P(("sweep", "na"), None, None, None, None)
    return jax.shard_map(
        per_device, mesh=mesh, in_specs=in_specs, out_specs=out_specs, check_vma=False
    )
```

```python
import functools
import jax
import jax.numpy as jnp
from jax import lax
from jax.experimental import pallas as pl
from jax.experimental.pallas import tpu as pltpu
from jax.sharding import PartitionSpec as P

step_size = 0.02
MESH = pl.DeviceIdType.MESH
NEAR, OWN, PARTNER, FAR, MID = 0, 1, 2, 3, 4
STRIP = 32
LAG = 2
EARLY = 3
PASS_DOWN = 1
FINAL, MIDDLE, SIDE, AHEAD, TOP = 0, 1, 2, 3, 4


def split(x):
    high = x.astype(jnp.bfloat16)
    return high, (x - high.astype(jnp.float32)).astype(jnp.bfloat16)


def kernel(
    total,
    order,
    hier_ref,
    ham_ref,
    coup_ref,
    damp_in,
    creal_in,
    cimag_in,
    out_ref,
    rho,
    w_left,
    w_right,
    x_left,
    x_right,
    table,
    ham_buf,
    damp_ref,
    creal_ref,
    cimag_ref,
    own_sem,
    ham_sem,
    small_sem,
    send_sem,
    recv_sem,
):
    M, N = order, total
    p = lax.axis_index("na")
    chip = p // 2
    core = p % 2
    odd = chip % 2
    chips = N // 2
    first = core == 0
    K = N - p
    pairs = N - 1 - 2 * chip

    is_relay = core != odd
    relays = jnp.logical_and(
        is_relay, jnp.where(odd == 1, chip >= 2, chip + 2 < chips)
    )
    fed_by_relay = jnp.logical_and(
        core == odd, jnp.where(odd == 1, chip + 2 < chips, chip >= 2)
    )
    direct_to = jnp.where(odd == 1, 2 * chip - 1, 2 * chip + 2)
    relay_to = jnp.where(odd == 1, p - 3, p + 3)
    relay_from = jnp.where(odd == 1, p + 3, p - 3)

    direct_count = jnp.where(p == 0, K - 4, jnp.where(p == 1, K - 2, K))
    near_count = jnp.where(first, jnp.where(p == 0, 0, K + 1), K - 1)
    near_count = jnp.where(p == 2, K - 1, near_count)
    far_count = jnp.where(
        first,
        jnp.where(
            p == 0, 0, jnp.where(jnp.logical_and(odd == 1, chip >= 2), K + 2, K)
        ),
        jnp.maximum(K - 2, 0),
    )
    far_count = jnp.where(p == 2, K - 2, far_count)
    relay_near_count = jnp.where(relays, jnp.where(first, near_count, K - 3), 0)
    relay_far_count = jnp.where(relays, far_count, 0)
    mid_near_count = jnp.where(first, jnp.where(p == 0, 0, K), K - 1)
    mid_near_count = jnp.where(p == 2, K - 2, mid_near_count)
    own_count = jnp.where(p == 2, K - 1, K)
    final_count = jnp.where(p == 2, K - 2, K)
    direct_slot = jnp.where(core == odd, FAR, NEAR)

    cut = N // 3
    one_ahead = N // 2
    none_ahead = N - 5

    def detour(i):
        return jnp.logical_and(i >= cut, i < cut + 2)

    def via_upper(i):
        return jnp.logical_and((p == 2) | (p == 3), detour(i))

    def direct_target(i):
        return jnp.where(via_upper(i), 4, direct_to)

    def elsewhere(i):
        return jnp.logical_and((p == 1) | (p == 4), detour(i))

    def waits_near(i):
        return jnp.logical_and(i < near_count, jnp.logical_not(elsewhere(i)))

    def waits_far(i):
        return jnp.logical_and(i < far_count, jnp.logical_not(elsewhere(i)))

    def passes_near(i):
        return jnp.logical_and(i < relay_near_count, jnp.logical_not(elsewhere(i)))

    def passes_far(i):
        return jnp.logical_and(i < relay_far_count, jnp.logical_not(elsewhere(i)))

    relay_to = jnp.where(p == 4, 1, relay_to)

    def own_copy(i):
        return pltpu.make_async_copy(
            hier_ref.at[0, i], rho.at[OWN, i], own_sem.at[i]
        )

    def operator_copy(k):
        return pltpu.make_async_copy(
            ham_ref if k == 0 else coup_ref.at[k - 1], ham_buf.at[k], ham_sem.at[k]
        )

    def remote(src, dst, send, recv, i, target):
        return pltpu.make_async_remote_copy(
            src_ref=src,
            dst_ref=dst,
            send_sem=send_sem.at[send, i],
            recv_sem=recv_sem.at[recv, i],
            device_id={"na": target},
            device_id_type=MESH,
        )

    def direct_copy(i):
        slot = jnp.where(via_upper(i), NEAR + FAR - direct_slot, direct_slot)
        return remote(
            hier_ref.at[0, i], rho.at[slot, i], 0, slot, i, direct_target(i)
        )

    def partner_copy(i):
        return remote(
            hier_ref.at[0, i], rho.at[PARTNER, i], 1, PARTNER, i, p + 1 - 2 * core
        )

    def relay_near(i):
        return remote(rho.at[NEAR, i], rho.at[FAR, i], 2, FAR, i, relay_to)

    def relay_far(i):
        return remote(rho.at[FAR, i], rho.at[NEAR, i], 3, NEAR, i, relay_to)

    def top_copy(i):
        return remote(rho.at[MID + FAR, i + 1], out_ref.at[0, i], 2, FAR, i, 2)

    def mid_copy(i):
        return remote(
            rho.at[MID + OWN, i], rho.at[MID + PARTNER, i], 4, 1, i, p + 1 - 2 * core
        )

    def arrival(which, i):
        return remote(
            rho.at[which, i], rho.at[which, i], 0, which, i, p + 1 - 2 * core
        )

    barrier = pltpu.get_barrier_semaphore()

    def greet(target):
        pl.semaphore_signal(
            barrier, inc=1, device_id={"na": target}, device_id_type=MESH
        )

    greet(p + 1 - 2 * core)
    greet(direct_to)

    @pl.when(is_relay)
    def _():
        greet(jnp.where(odd == 1, p - 2, p + 2))

    @pl.when(relays)
    def _():
        greet(relay_to)

    @pl.when(fed_by_relay)
    def _():
        greet(relay_from)

    for one, other in ((2, 4), (3, 4)):
        for me, peer in ((one, other), (other, one)):

            @pl.when(p == me)
            def _(peer=peer):
                greet(peer)

    pl.semaphore_wait(
        barrier,
        2
        + jnp.where(jnp.logical_or(p == 2, p == 3), 1, 0)
        + jnp.where(p == 4, 2, 0)
        + is_relay.astype(jnp.int32)
        + relays.astype(jnp.int32)
        + fed_by_relay.astype(jnp.int32),
    )

    @pl.loop(0, K)
    def _(i):
        @pl.when(i < direct_count)
        def _():
            direct_copy(i).start()

        @pl.when(i < pairs)
        def _():
            partner_copy(i).start()

    small = [
        pltpu.make_async_copy(source, target, small_sem.at[k])
        for k, (source, target) in enumerate(
            ((damp_in, damp_ref), (creal_in, creal_ref), (cimag_in, cimag_ref))
        )
    ]
    for k in range(3):
        small[k].start()
        operator_copy(k).start()

    @pl.loop(0, K)
    def _(i):
        own_copy(i).start()

    for k in range(3):
        operator_copy(k).wait()
        raw = ham_buf[k]
        high, low = split(0.5 * (raw + raw.T))
        for half in range(2):
            cols = slice((3 * half + k) * M, (3 * half + k + 1) * M)
            w_left[0:M, cols] = high
            w_left[M : 2 * M, cols] = low
            w_right[cols, 0:M] = high
            w_right[cols, M : 2 * M] = low

    for copy in small:
        copy.wait()

    for mode in range(2):
        re = jnp.full((8, M), creal_ref[mode], jnp.float32)
        im = jnp.full((8, M), cimag_ref[mode], jnp.float32)
        magnitude = jnp.sqrt(re * re + im * im)

        @pl.loop(0, N)
        def _(n):
            occupied = jnp.full((8, M), n.astype(jnp.float32), jnp.float32)
            lower = jnp.sqrt(occupied / magnitude)
            table[3 * mode, n] = jnp.sqrt((occupied + 1.0) * magnitude)
            table[3 * mode + 1, n] = lower * re
            table[3 * mode + 2, n] = lower * im

    @pl.loop(K, N)
    def _(i):
        out_ref[0, i] = jnp.zeros((2, M, M), jnp.float32)

    def advance(own, up, down, q, n, base, scale, store):
        alive = q + n < N - 1
        alive_scale = jnp.where(alive, 1.0, 0.0)
        up = jnp.where(alive, up, own)
        above = jnp.where(alive, n + 1, n)
        below = jnp.maximum(n - 1, 0)

        def put(block, rows, part, x, is_left):
            high, low = split(x)
            for half, value in ((0, high), (1, low)):
                at = (3 * half + block) * M
                if is_left:
                    x_left[
                        at + rows : at + rows + STRIP, part * M : (part + 1) * M
                    ] = value
                else:
                    x_right[
                        part * M + rows : part * M + rows + STRIP, at : at + M
                    ] = value

        for rows in range(0, M, STRIP):
            strip = slice(rows, rows + STRIP)
            for part in range(2):
                value = rho[own, n, part, strip, :]
                put(0, rows, part, value, True)
                put(0, rows, part, value, False)
            for mode, occupied, (ub, us), (vb, vs) in (
                (0, q, (up, n), (down, n)),
                (1, n, (own, above), (own, below)),
            ):
                raise_w = table[3 * mode, occupied, 0:1, :] * alive_scale
                direct_w = table[3 * mode + 1, occupied, 0:1, :]
                cross_w = table[3 * mode + 2, occupied, 0:1, :]
                v_re = rho[vb, vs, 0, strip, :]
                v_im = rho[vb, vs, 1, strip, :]
                e_re = raise_w * rho[ub, us, 0, strip, :] + direct_w * v_re
                e_im = raise_w * rho[ub, us, 1, strip, :] + direct_w * v_im
                x_re = cross_w * v_im
                x_im = cross_w * v_re
                put(1 + mode, rows, 0, e_re - x_re, True)
                put(1 + mode, rows, 0, e_re + x_re, False)
                put(1 + mode, rows, 1, e_im + x_im, True)
                put(1 + mode, rows, 1, e_im - x_im, False)
        left = jnp.dot(w_left[...], x_left[...], preferred_element_type=jnp.float32)
        right = jnp.dot(x_right[...], w_right[...], preferred_element_type=jnp.float32)
        damping = (
            q.astype(jnp.float32) * damp_ref[0] + n.astype(jnp.float32) * damp_ref[1]
        )
        left = left[0:M] + left[M : 2 * M]
        right = right[:, 0:M] + right[:, M : 2 * M]
        change_re = left[:, M : 2 * M] - right[M : 2 * M] - damping * rho[own, n, 0]
        change_im = right[0:M] - left[:, 0:M] - damping * rho[own, n, 1]
        store(rho[base, n, 0] + scale * change_re, rho[base, n, 1] + scale * change_im)

    up = jnp.where(first, PARTNER, NEAR)
    down = jnp.where(first, jnp.where(p == 0, OWN, NEAR), PARTNER)
    near_up = jnp.where(first, OWN, FAR)
    near_down = jnp.where(first, FAR, OWN)
    near_q = jnp.where(first, p - 1, p + 1)

    def take(i):
        @pl.when(waits_near(i))
        def _():
            arrival(NEAR, i).wait_recv()

        @pl.when(passes_near(i))
        def _():
            relay_near(i).start()

        @pl.when(waits_far(i))
        def _():
            arrival(FAR, i).wait_recv()

        @pl.when(passes_far(i))
        def _():
            relay_far(i).start()

    early = jnp.logical_and(core == 1, K - 1 > EARLY + 1)
    in_turn = jnp.where(early, K - 1, own_count)

    @pl.loop(0, K)
    def _(i):
        own_copy(i).wait()

    lag = jnp.where(jnp.logical_and(relays, p != 1), LAG, 1)

    @pl.loop(-1, K + lag)
    def _(i):
        j = i - lag
        ahead = jnp.logical_and(early, i == EARLY)

        top = jnp.logical_and(p == 1, i == K - 2)

        @pl.loop(0, jnp.where(top, 7, jnp.where(ahead, 4, 3)))
        def _(turn):
            kind = jnp.where(top, lax.rem(turn + 1, 7), turn)
            is_final = kind == FINAL
            is_near = kind == SIDE

            @pl.when(jnp.logical_and(is_final, jnp.logical_and(j >= 0, j < pairs)))
            def _():
                mid_copy(j).wait_recv()

            @pl.when(kind == MIDDLE)
            def _():
                @pl.when(jnp.logical_and(p == 4, i == PASS_DOWN))
                def _():
                    for k in (cut, cut + 1):
                        arrival(FAR, k).wait_recv()
                        relay_far(k).start()
                        arrival(NEAR, k).wait_recv()
                        relay_near(k).start()

                c = i + 1
                extra = jnp.where(c < one_ahead, 2, jnp.where(c < none_ahead, 1, 0))
                extra = jnp.where(jnp.logical_or(p != 1, c < cut), 0, extra)
                skip = (p == 1) & ((c == one_ahead) | (c == none_ahead))

                @pl.when(jnp.logical_not(skip))
                def _():
                    take(c + extra)

                @pl.when(jnp.logical_and(p == 1, detour(c)))
                def _():
                    arrival(NEAR, c).wait_recv()
                    arrival(FAR, c).wait_recv()

                @pl.when(jnp.logical_and(i < EARLY, i + 1 < pairs))
                def _():
                    arrival(PARTNER, i + 1).wait_recv()

                @pl.when(i == EARLY)
                def _():
                    @pl.loop(EARLY + 1, pairs)
                    def _(k):
                        arrival(PARTNER, k).wait_recv()

            is_own = jnp.logical_or(kind == MIDDLE, kind == AHEAD)
            is_top = kind > TOP
            n = jnp.where(kind == FINAL, j, jnp.where(kind == SIDE, i, i + 1))
            n = jnp.where(kind == AHEAD, K - 1, n)
            n = jnp.where(kind == TOP + 1, N - 3, jnp.where(kind >= TOP, N - 4, n))
            limit = jnp.where(is_final, final_count, mid_near_count)
            limit = jnp.where(kind == MIDDLE, in_turn, limit)
            limit = jnp.where(kind == AHEAD, jnp.where(ahead, K, 0), limit)
            limit = jnp.where(kind >= TOP, N, limit)

            @pl.when(jnp.logical_and(n >= 0, n < limit))
            def _():
                shift = jnp.where(jnp.logical_or(is_final, is_top), MID, 0)
                source = jnp.where(
                    kind == TOP, FAR, jnp.where(is_near | is_top, NEAR, OWN)
                )
                above = jnp.where(is_near, near_up, up)
                above = jnp.where(kind >= TOP, FAR, above)
                below = jnp.where(is_near, near_down, down)
                below = jnp.where(kind == TOP, NEAR, jnp.where(is_top, OWN, below))
                row = jnp.where(is_near, near_q, p)
                row = jnp.where(kind == TOP, p + 2, jnp.where(is_top, p + 1, row))

                def store(real, imag):
                    @pl.when(is_final)
                    def _():
                        out_ref[0, n, 0] = real
                        out_ref[0, n, 1] = imag

                    @pl.when(jnp.logical_not(is_final))
                    def _():
                        into = MID + jnp.where(is_top, FAR, source)
                        at = jnp.where(is_top, n + 1, n)
                        rho[into, at, 0] = real
                        rho[into, at, 1] = imag

                advance(
                    shift + source,
                    shift + above,
                    shift + below,
                    row,
                    n,
                    source,
                    jnp.where(shift > 0, step_size, 0.5 * step_size),
                    store,
                )

                @pl.when(jnp.logical_and(is_own, n < pairs))
                def _():
                    mid_copy(n).start()

                @pl.when(is_top)
                def _():
                    top_copy(n).start()

    @pl.when(p == 1)
    def _():
        for i in range(N - 4, N - 2):
            top_copy(i).wait_send()

    @pl.when(p == 2)
    def _():
        for i in range(N - 4, N - 2):
            top_copy(i).wait_recv()

    @pl.loop(0, N)
    def _(i):
        @pl.when(i < direct_count)
        def _():
            direct_copy(i).wait_send()

        @pl.when(i < pairs)
        def _():
            partner_copy(i).wait_send()
            mid_copy(i).wait_send()

        @pl.when(passes_near(i) | (p == 4) & detour(i))
        def _():
            relay_near(i).wait_send()

        @pl.when(passes_far(i) | (p == 4) & detour(i))
        def _():
            relay_far(i).wait_send()


def per_device(hierarchy, hamiltonian, couplings, damp_rates, coef_real, coef_imag):
    total = hierarchy.shape[1]
    M = hierarchy.shape[-1]
    hbm = pl.BlockSpec(memory_space=pltpu.HBM)
    return pl.pallas_call(
        functools.partial(kernel, total, M),
        out_shape=pltpu.VMEM(hierarchy.shape, jnp.float32),
        in_specs=[hbm] * 6,
        out_specs=pl.BlockSpec(memory_space=pltpu.VMEM),
        scratch_shapes=[
            pltpu.VMEM((MID + 4, total, 2, M, M), jnp.float32),
            pltpu.VMEM((2 * M, 6 * M), jnp.bfloat16),
            pltpu.VMEM((6 * M, 2 * M), jnp.bfloat16),
            pltpu.VMEM((6 * M, 2 * M), jnp.bfloat16),
            pltpu.VMEM((2 * M, 6 * M), jnp.bfloat16),
            pltpu.VMEM((6, total, 8, M), jnp.float32),
            pltpu.VMEM((3, M, M), jnp.float32),
            pltpu.SMEM(damp_rates.shape, jnp.float32),
            pltpu.SMEM(coef_real.shape, jnp.float32),
            pltpu.SMEM(coef_imag.shape, jnp.float32),
            pltpu.SemaphoreType.DMA((total,)),
            pltpu.SemaphoreType.DMA((3,)),
            pltpu.SemaphoreType.DMA((3,)),
            pltpu.SemaphoreType.DMA((5, total)),
            pltpu.SemaphoreType.DMA((4, total)),
        ],
        compiler_params=pltpu.CompilerParams(
            collective_id=0, has_side_effects=True, vmem_limit_bytes=(8 + total) * 2**20
        ),
    )(
        *(
            pltpu.with_memory_space_constraint(x, pltpu.HBM)
            for x in (
                hierarchy,
                hamiltonian,
                couplings,
                damp_rates,
                coef_real,
                coef_imag,
            )
        )
    )


def solution(mesh):
    in_specs = (
        P(("sweep", "na"), None, None, None, None),
        P(),
        P(),
        P("sweep"),
        P("sweep"),
        P("sweep"),
    )
    out_specs = P(("sweep", "na"), None, None, None, None)
    return jax.shard_map(
        per_device, mesh=mesh, in_specs=in_specs, out_specs=out_specs, check_vma=False
    )
```

```python
import functools
import jax
import jax.numpy as jnp
from jax import lax
from jax.experimental import pallas as pl
from jax.experimental.pallas import tpu as pltpu
from jax.sharding import PartitionSpec as P

step_size = 0.02
MESH = pl.DeviceIdType.MESH
NEAR, OWN, PARTNER, FAR, MID = 0, 1, 2, 3, 4
STRIP = 32
LAG = 2
EARLY = 3
PASS_DOWN = 1
FINAL, MIDDLE, SIDE, AHEAD, TOP = 0, 1, 2, 3, 4


def split(x):
    high = x.astype(jnp.bfloat16)
    return high, (x - high.astype(jnp.float32)).astype(jnp.bfloat16)


def kernel(
    total,
    order,
    hier_ref,
    ham_ref,
    coup_ref,
    damp_in,
    creal_in,
    cimag_in,
    out_ref,
    rho,
    w_left,
    w_right,
    x_left,
    x_right,
    table,
    ham_buf,
    damp_ref,
    creal_ref,
    cimag_ref,
    own_sem,
    ham_sem,
    small_sem,
    send_sem,
    recv_sem,
):
    M, N = order, total
    p = lax.axis_index("na")
    chip = p // 2
    core = p % 2
    odd = chip % 2
    chips = N // 2
    first = core == 0
    K = N - p
    pairs = N - 1 - 2 * chip

    is_relay = core != odd
    relays = jnp.logical_and(
        is_relay, jnp.where(odd == 1, chip >= 2, chip + 2 < chips)
    )
    fed_by_relay = jnp.logical_and(
        core == odd, jnp.where(odd == 1, chip + 2 < chips, chip >= 2)
    )
    direct_to = jnp.where(odd == 1, 2 * chip - 1, 2 * chip + 2)
    relay_to = jnp.where(odd == 1, p - 3, p + 3)
    relay_from = jnp.where(odd == 1, p + 3, p - 3)

    direct_count = jnp.where(p == 0, K - 4, jnp.where(p == 1, K - 2, K))
    near_count = jnp.where(first, jnp.where(p == 0, 0, K + 1), K - 1)
    near_count = jnp.where(p == 2, K - 1, near_count)
    far_count = jnp.where(
        first,
        jnp.where(
            p == 0, 0, jnp.where(jnp.logical_and(odd == 1, chip >= 2), K + 2, K)
        ),
        jnp.maximum(K - 2, 0),
    )
    far_count = jnp.where(p == 2, K - 2, far_count)
    relay_near_count = jnp.where(relays, jnp.where(first, near_count, K - 3), 0)
    relay_far_count = jnp.where(relays, far_count, 0)
    mid_near_count = jnp.where(first, jnp.where(p == 0, 0, K), K - 1)
    mid_near_count = jnp.where(p == 2, K - 2, mid_near_count)
    own_count = jnp.where(p == 2, K - 1, K)
    final_count = jnp.where(p == 2, K - 2, K)
    direct_slot = jnp.where(core == odd, FAR, NEAR)

    cut = N // 3
    one_ahead = N // 2
    none_ahead = N - 5

    def detour(i):
        return jnp.logical_and(i >= cut, i < cut + 2)

    def via_upper(i):
        return jnp.logical_and((p == 2) | (p == 3), detour(i))

    def direct_target(i):
        return jnp.where(via_upper(i), 4, direct_to)

    def elsewhere(i):
        return jnp.logical_and((p == 1) | (p == 4), detour(i))

    def waits_near(i):
        return jnp.logical_and(i < near_count, jnp.logical_not(elsewhere(i)))

    def waits_far(i):
        return jnp.logical_and(i < far_count, jnp.logical_not(elsewhere(i)))

    def passes_near(i):
        return jnp.logical_and(i < relay_near_count, jnp.logical_not(elsewhere(i)))

    def passes_far(i):
        return jnp.logical_and(i < relay_far_count, jnp.logical_not(elsewhere(i)))

    relay_to = jnp.where(p == 4, 1, relay_to)

    def own_copy():
        return pltpu.make_async_copy(hier_ref.at[0], rho.at[OWN], own_sem.at[0])

    def operator_copy(k):
        return pltpu.make_async_copy(
            ham_ref if k == 0 else coup_ref.at[k - 1], ham_buf.at[k], ham_sem.at[k]
        )

    def remote(src, dst, send, recv, i, target):
        return pltpu.make_async_remote_copy(
            src_ref=src,
            dst_ref=dst,
            send_sem=send_sem.at[send, i],
            recv_sem=recv_sem.at[recv - recv // 3, i],
            device_id={"na": target},
            device_id_type=MESH,
        )

    def direct_copy(i):
        slot = jnp.where(via_upper(i), NEAR + FAR - direct_slot, direct_slot)
        return remote(
            hier_ref.at[0, i], rho.at[slot, i], 0, slot, i, direct_target(i)
        )

    def partner_copy():
        return pltpu.make_async_remote_copy(
            src_ref=hier_ref.at[0],
            dst_ref=rho.at[PARTNER],
            send_sem=own_sem.at[1],
            recv_sem=own_sem.at[2],
            device_id={"na": p + 1 - 2 * core},
            device_id_type=MESH,
        )

    def relay_near(i):
        return remote(rho.at[NEAR, i], rho.at[FAR, i], 2, FAR, i, relay_to)

    def relay_far(i):
        return remote(rho.at[FAR, i], rho.at[NEAR, i], 3, NEAR, i, relay_to)

    def top_copy(i):
        return remote(rho.at[MID + FAR, i + 1], out_ref.at[0, i], 2, FAR, i, 2)

    def mid_copy(i):
        return remote(
            rho.at[MID + OWN, i], rho.at[MID + PARTNER, i], 1, OWN, i, p + 1 - 2 * core
        )

    def arrival(which, i):
        return remote(
            rho.at[which, i], rho.at[which, i], 0, which, i, p + 1 - 2 * core
        )

    barrier = pltpu.get_barrier_semaphore()

    def greet(target):
        pl.semaphore_signal(
            barrier, inc=1, device_id={"na": target}, device_id_type=MESH
        )

    greet(p + 1 - 2 * core)
    greet(direct_to)

    @pl.when(is_relay)
    def _():
        greet(jnp.where(odd == 1, p - 2, p + 2))

    @pl.when(relays)
    def _():
        greet(relay_to)

    @pl.when(fed_by_relay)
    def _():
        greet(relay_from)

    for one, other in ((2, 4), (3, 4)):
        for me, peer in ((one, other), (other, one)):

            @pl.when(p == me)
            def _(peer=peer):
                greet(peer)

    pl.semaphore_wait(
        barrier,
        2
        + jnp.where(jnp.logical_or(p == 2, p == 3), 1, 0)
        + jnp.where(p == 4, 2, 0)
        + is_relay.astype(jnp.int32)
        + relays.astype(jnp.int32)
        + fed_by_relay.astype(jnp.int32),
    )

    direct_copy(0).start()
    partner_copy().start()

    @pl.loop(1, direct_count)
    def _(i):
        direct_copy(i).start()

    small = [
        pltpu.make_async_copy(source, target, small_sem.at[k])
        for k, (source, target) in enumerate(
            ((damp_in, damp_ref), (creal_in, creal_ref), (cimag_in, cimag_ref))
        )
    ]
    for k in range(3):
        small[k].start()
        operator_copy(k).start()

    own_copy().start()

    for k in range(3):
        operator_copy(k).wait()
        raw = ham_buf[k]
        high, low = split(0.5 * (raw + raw.T))
        for half in range(2):
            cols = slice((3 * half + k) * M, (3 * half + k + 1) * M)
            w_left[0:M, cols] = high
            w_left[M : 2 * M, cols] = low
            w_right[cols, 0:M] = high
            w_right[cols, M : 2 * M] = low

    for copy in small:
        copy.wait()

    for mode in range(2):
        re = jnp.full((8, M), creal_ref[mode], jnp.float32)
        im = jnp.full((8, M), cimag_ref[mode], jnp.float32)
        magnitude = jnp.sqrt(re * re + im * im)

        @pl.loop(0, N)
        def _(n):
            occupied = jnp.full((8, M), n.astype(jnp.float32), jnp.float32)
            lower = jnp.sqrt(occupied / magnitude)
            table[3 * mode, n] = jnp.sqrt((occupied + 1.0) * magnitude)
            table[3 * mode + 1, n] = lower * re
            table[3 * mode + 2, n] = lower * im

    @pl.loop(K, N)
    def _(i):
        out_ref[0, i] = jnp.zeros((2, M, M), jnp.float32)

    def build(task, own, up, down, q, n):
        alive = q + n < N - 1
        alive_scale = jnp.where(alive, 1.0, 0.0)
        up = jnp.where(alive, up, own)
        above = jnp.where(alive, n + 1, n)
        below = jnp.maximum(n - 1, 0)

        def put(block, rows, part, x, is_left):
            high, low = split(x)
            across = (2 * task + part) * M
            for half, value in ((0, high), (1, low)):
                at = (3 * half + block) * M
                if is_left:
                    x_left[at + rows : at + rows + STRIP, across : across + M] = value
                else:
                    x_right[across + rows : across + rows + STRIP, at : at + M] = value

        for rows in range(0, M, STRIP):
            strip = slice(rows, rows + STRIP)
            for part in range(2):
                value = rho[own, n, part, strip, :]
                put(0, rows, part, value, True)
                put(0, rows, part, value, False)
            for mode, occupied, (ub, us), (vb, vs) in (
                (0, q, (up, n), (down, n)),
                (1, n, (own, above), (own, below)),
            ):
                raise_w = table[3 * mode, occupied, 0:1, :] * alive_scale
                direct_w = table[3 * mode + 1, occupied, 0:1, :]
                cross_w = table[3 * mode + 2, occupied, 0:1, :]
                v_re = rho[vb, vs, 0, strip, :]
                v_im = rho[vb, vs, 1, strip, :]
                e_re = raise_w * rho[ub, us, 0, strip, :] + direct_w * v_re
                e_im = raise_w * rho[ub, us, 1, strip, :] + direct_w * v_im
                x_re = cross_w * v_im
                x_im = cross_w * v_re
                put(1 + mode, rows, 0, e_re - x_re, True)
                put(1 + mode, rows, 0, e_re + x_re, False)
                put(1 + mode, rows, 1, e_im + x_im, True)
                put(1 + mode, rows, 1, e_im - x_im, False)

    def advance(tasks):
        for task, (own, up, down, q, n, base, scale, store) in enumerate(tasks):
            build(task, own, up, down, q, n)
        wide = 2 * M * len(tasks)
        lefts = jnp.dot(
            w_left[...], x_left[:, 0:wide], preferred_element_type=jnp.float32
        )
        rights = jnp.dot(
            x_right[0:wide, :], w_right[...], preferred_element_type=jnp.float32
        )
        for task, (own, up, down, q, n, base, scale, store) in enumerate(tasks):
            damping = (
                q.astype(jnp.float32) * damp_ref[0] + n.astype(jnp.float32) * damp_ref[1]
            )
            across = slice(2 * M * task, 2 * M * (task + 1))
            left = lefts[0:M, across] + lefts[M : 2 * M, across]
            right = rights[across, 0:M] + rights[across, M : 2 * M]
            change_re = left[:, M : 2 * M] - right[M : 2 * M] - damping * rho[own, n, 0]
            change_im = right[0:M] - left[:, 0:M] - damping * rho[own, n, 1]
            store(
                rho[base, n, 0] + scale * change_re, rho[base, n, 1] + scale * change_im
            )

    up = jnp.where(first, PARTNER, NEAR)
    down = jnp.where(first, jnp.where(p == 0, OWN, NEAR), PARTNER)
    near_up = jnp.where(first, OWN, FAR)
    near_down = jnp.where(first, FAR, OWN)
    near_q = jnp.where(first, p - 1, p + 1)

    def take(i):
        @pl.when(waits_near(i))
        def _():
            arrival(NEAR, i).wait_recv()

        @pl.when(passes_near(i))
        def _():
            relay_near(i).start()

        @pl.when(waits_far(i))
        def _():
            arrival(FAR, i).wait_recv()

        @pl.when(passes_far(i))
        def _():
            relay_far(i).start()

    early = jnp.logical_and(core == 1, K - 1 > EARLY + 1)
    in_turn = jnp.where(early, K - 1, own_count)

    own_copy().wait()

    lag = jnp.where(jnp.logical_and(relays, p != 1), LAG, 1)

    @pl.loop(-1, K + lag)
    def _(i):
        j = i - lag
        ahead = jnp.logical_and(early, i == EARLY)

        top = jnp.logical_and(p == 1, i == K - 2)

        @pl.loop(0, jnp.where(top, 7, jnp.where(ahead, 4, 3)))
        def _(turn):
            kind = jnp.where(top, lax.rem(turn + 1, 7), turn)
            is_final = kind == FINAL
            is_near = kind == SIDE

            @pl.when(jnp.logical_and(is_final, jnp.logical_and(j >= 0, j < pairs)))
            def _():
                mid_copy(j).wait_recv()

            @pl.when(kind == MIDDLE)
            def _():
                @pl.when(jnp.logical_and(p == 4, i == PASS_DOWN))
                def _():
                    for k in (cut, cut + 1):
                        arrival(FAR, k).wait_recv()
                        relay_far(k).start()
                        arrival(NEAR, k).wait_recv()
                        relay_near(k).start()

                c = i + 1
                extra = jnp.where(c < one_ahead, 2, jnp.where(c < none_ahead, 1, 0))
                extra = jnp.where(jnp.logical_or(p != 1, c < cut), 0, extra)
                skip = (p == 1) & ((c == one_ahead) | (c == none_ahead))

                @pl.when(jnp.logical_not(skip))
                def _():
                    take(c + extra)

                @pl.when(jnp.logical_and(p == 1, detour(c)))
                def _():
                    arrival(NEAR, c).wait_recv()
                    arrival(FAR, c).wait_recv()

                @pl.when(c == 0)
                def _():
                    partner_copy().wait_recv()

            is_own = jnp.logical_or(kind == MIDDLE, kind == AHEAD)
            is_top = kind > TOP
            n = jnp.where(kind == FINAL, j, jnp.where(kind == SIDE, i, i + 1))
            n = jnp.where(kind == AHEAD, K - 1, n)
            n = jnp.where(kind == TOP + 1, N - 3, jnp.where(kind >= TOP, N - 4, n))
            limit = jnp.where(is_final, final_count, mid_near_count)
            limit = jnp.where(kind == MIDDLE, in_turn, limit)
            limit = jnp.where(kind == AHEAD, jnp.where(ahead, K, 0), limit)
            limit = jnp.where(kind >= TOP, N, limit)
            both = (i + 1 < in_turn) & (i >= 0) & (i < mid_near_count)
            limit = jnp.where(both & ((kind == MIDDLE) | (kind == SIDE)), 0, limit)

            @pl.when(both & (kind == MIDDLE))
            def _():
                def keep(slot, at):
                    def store(real, imag):
                        rho[slot, at, 0] = real
                        rho[slot, at, 1] = imag

                    return store

                half = 0.5 * step_size
                advance(
                    [
                        (OWN, up, down, p, n, OWN, half, keep(MID + OWN, n)),
                        (
                            NEAR,
                            near_up,
                            near_down,
                            near_q,
                            i,
                            NEAR,
                            half,
                            keep(MID + NEAR, i),
                        ),
                    ]
                )

                @pl.when(n < pairs)
                def _():
                    mid_copy(n).start()


            @pl.when(jnp.logical_and(n >= 0, n < limit))
            def _():
                shift = jnp.where(jnp.logical_or(is_final, is_top), MID, 0)
                source = jnp.where(
                    kind == TOP, FAR, jnp.where(is_near | is_top, NEAR, OWN)
                )
                above = jnp.where(is_near, near_up, up)
                above = jnp.where(kind >= TOP, FAR, above)
                below = jnp.where(is_near, near_down, down)
                below = jnp.where(kind == TOP, NEAR, jnp.where(is_top, OWN, below))
                row = jnp.where(is_near, near_q, p)
                row = jnp.where(kind == TOP, p + 2, jnp.where(is_top, p + 1, row))

                def store(real, imag):
                    @pl.when(is_final)
                    def _():
                        out_ref[0, n, 0] = real
                        out_ref[0, n, 1] = imag

                    @pl.when(jnp.logical_not(is_final))
                    def _():
                        into = MID + jnp.where(is_top, FAR, source)
                        at = jnp.where(is_top, n + 1, n)
                        rho[into, at, 0] = real
                        rho[into, at, 1] = imag

                advance(
                    [
                        (
                            shift + source,
                            shift + above,
                            shift + below,
                            row,
                            n,
                            source,
                            jnp.where(shift > 0, step_size, 0.5 * step_size),
                            store,
                        )
                    ]
                )

                @pl.when(jnp.logical_and(is_own, n < pairs))
                def _():
                    mid_copy(n).start()

                @pl.when(is_top)
                def _():
                    top_copy(n).start()

    @pl.when(p == 1)
    def _():
        for i in range(N - 4, N - 2):
            top_copy(i).wait_send()

    @pl.when(p == 2)
    def _():
        for i in range(N - 4, N - 2):
            top_copy(i).wait_recv()

    partner_copy().wait_send()

    @pl.loop(0, N)
    def _(i):
        @pl.when(i < direct_count)
        def _():
            direct_copy(i).wait_send()

        @pl.when(i < pairs)
        def _():
            mid_copy(i).wait_send()

        @pl.when(passes_near(i) | (p == 4) & detour(i))
        def _():
            relay_near(i).wait_send()

        @pl.when(passes_far(i) | (p == 4) & detour(i))
        def _():
            relay_far(i).wait_send()


def per_device(hierarchy, hamiltonian, couplings, damp_rates, coef_real, coef_imag):
    total = hierarchy.shape[1]
    M = hierarchy.shape[-1]
    hbm = pl.BlockSpec(memory_space=pltpu.HBM)
    return pl.pallas_call(
        functools.partial(kernel, total, M),
        out_shape=pltpu.VMEM(hierarchy.shape, jnp.float32),
        in_specs=[hbm] * 6,
        out_specs=pl.BlockSpec(memory_space=pltpu.VMEM),
        scratch_shapes=[
            pltpu.VMEM((MID + 4, total, 2, M, M), jnp.float32),
            pltpu.VMEM((2 * M, 6 * M), jnp.bfloat16),
            pltpu.VMEM((6 * M, 2 * M), jnp.bfloat16),
            pltpu.VMEM((6 * M, 4 * M), jnp.bfloat16),
            pltpu.VMEM((4 * M, 6 * M), jnp.bfloat16),
            pltpu.VMEM((6, total, 8, M), jnp.float32),
            pltpu.VMEM((3, M, M), jnp.float32),
            pltpu.SMEM(damp_rates.shape, jnp.float32),
            pltpu.SMEM(coef_real.shape, jnp.float32),
            pltpu.SMEM(coef_imag.shape, jnp.float32),
            pltpu.SemaphoreType.DMA((3,)),
            pltpu.SemaphoreType.DMA((3,)),
            pltpu.SemaphoreType.DMA((3,)),
            pltpu.SemaphoreType.DMA((4, total)),
            pltpu.SemaphoreType.DMA((3, total)),
        ],
        compiler_params=pltpu.CompilerParams(
            collective_id=0, has_side_effects=True, vmem_limit_bytes=(8 + total) * 2**20
        ),
    )(
        *(
            pltpu.with_memory_space_constraint(x, pltpu.HBM)
            for x in (
                hierarchy,
                hamiltonian,
                couplings,
                damp_rates,
                coef_real,
                coef_imag,
            )
        )
    )


def solution(mesh):
    in_specs = (
        P(("sweep", "na"), None, None, None, None),
        P(),
        P(),
        P("sweep"),
        P("sweep"),
        P("sweep"),
    )
    out_specs = P(("sweep", "na"), None, None, None, None)
    return jax.shard_map(
        per_device, mesh=mesh, in_specs=in_specs, out_specs=out_specs, check_vma=False
    )
```

```python
import functools
import jax
import jax.numpy as jnp
from jax import lax
from jax.experimental import pallas as pl
from jax.experimental.pallas import tpu as pltpu
from jax.sharding import PartitionSpec as P

step_size = 0.02
MESH = pl.DeviceIdType.MESH
NEAR, OWN, PARTNER, FAR, MID = 0, 1, 2, 3, 4
STRIP = 32
LAG = 2
EARLY = 3
PASS_DOWN = 1
FINAL, MIDDLE, SIDE, AHEAD, TOP = 0, 1, 2, 3, 4


def split(x):
    high = x.astype(jnp.bfloat16)
    return high, (x - high.astype(jnp.float32)).astype(jnp.bfloat16)


def kernel(
    total,
    order,
    hier_ref,
    ham_ref,
    coup_ref,
    damp_in,
    creal_in,
    cimag_in,
    out_ref,
    rho,
    w_left,
    w_right,
    x_left,
    x_right,
    table,
    ham_buf,
    damp_ref,
    creal_ref,
    cimag_ref,
    own_sem,
    ham_sem,
    small_sem,
    send_sem,
    recv_sem,
):
    M, N = order, total
    p = lax.axis_index("na")
    chip = p // 2
    core = p % 2
    odd = chip % 2
    chips = N // 2
    first = core == 0
    K = N - p
    pairs = N - 1 - 2 * chip

    is_relay = core != odd
    relays = jnp.logical_and(
        is_relay, jnp.where(odd == 1, chip >= 2, chip + 2 < chips)
    )
    fed_by_relay = jnp.logical_and(
        core == odd, jnp.where(odd == 1, chip + 2 < chips, chip >= 2)
    )
    direct_to = jnp.where(odd == 1, 2 * chip - 1, 2 * chip + 2)
    relay_to = jnp.where(odd == 1, p - 3, p + 3)
    relay_from = jnp.where(odd == 1, p + 3, p - 3)

    direct_count = jnp.where(p == 0, K - 4, jnp.where(p == 1, K - 2, K))
    near_count = jnp.where(first, jnp.where(p == 0, 0, K + 1), K - 1)
    near_count = jnp.where(p == 2, K - 1, near_count)
    far_count = jnp.where(
        first,
        jnp.where(
            p == 0, 0, jnp.where(jnp.logical_and(odd == 1, chip >= 2), K + 2, K)
        ),
        jnp.maximum(K - 2, 0),
    )
    far_count = jnp.where(p == 2, K - 2, far_count)
    relay_near_count = jnp.where(relays, jnp.where(first, near_count, K - 3), 0)
    relay_far_count = jnp.where(relays, far_count, 0)
    mid_near_count = jnp.where(first, jnp.where(p == 0, 0, K), K - 1)
    mid_near_count = jnp.where(p == 2, K - 2, mid_near_count)
    own_count = jnp.where(p == 2, K - 1, K)
    final_count = jnp.where(p == 2, K - 2, K)
    direct_slot = jnp.where(core == odd, FAR, NEAR)

    cut = N // 3
    one_ahead = N // 2
    none_ahead = N - 5

    def detour(i):
        return jnp.logical_and(i >= cut, i < cut + 2)

    def via_upper(i):
        return jnp.logical_and((p == 2) | (p == 3), detour(i))

    def direct_target(i):
        return jnp.where(via_upper(i), 4, direct_to)

    def elsewhere(i):
        return jnp.logical_and((p == 1) | (p == 4), detour(i))

    def waits_near(i):
        return jnp.logical_and(i < near_count, jnp.logical_not(elsewhere(i)))

    def waits_far(i):
        return jnp.logical_and(i < far_count, jnp.logical_not(elsewhere(i)))

    def passes_near(i):
        return jnp.logical_and(i < relay_near_count, jnp.logical_not(elsewhere(i)))

    def passes_far(i):
        return jnp.logical_and(i < relay_far_count, jnp.logical_not(elsewhere(i)))

    relay_to = jnp.where(p == 4, 1, relay_to)

    def own_copy():
        return pltpu.make_async_copy(hier_ref.at[0], rho.at[OWN], own_sem.at[0])

    def operator_copy(k):
        return pltpu.make_async_copy(
            ham_ref if k == 0 else coup_ref.at[k - 1], ham_buf.at[k], ham_sem.at[k]
        )

    def remote(src, dst, send, recv, i, target):
        return pltpu.make_async_remote_copy(
            src_ref=src,
            dst_ref=dst,
            send_sem=send_sem.at[send],
            recv_sem=recv_sem.at[recv - recv // 3, i],
            device_id={"na": target},
            device_id_type=MESH,
        )

    def direct_copy(i):
        slot = jnp.where(via_upper(i), NEAR + FAR - direct_slot, direct_slot)
        return remote(
            hier_ref.at[0, i], rho.at[slot, i], 0, slot, i, direct_target(i)
        )

    def partner_copy():
        return pltpu.make_async_remote_copy(
            src_ref=hier_ref.at[0],
            dst_ref=rho.at[PARTNER],
            send_sem=own_sem.at[1],
            recv_sem=own_sem.at[2],
            device_id={"na": p + 1 - 2 * core},
            device_id_type=MESH,
        )

    def relay_near(i):
        return remote(rho.at[NEAR, i], rho.at[FAR, i], 2, FAR, i, relay_to)

    def relay_far(i):
        return remote(rho.at[FAR, i], rho.at[NEAR, i], 3, NEAR, i, relay_to)

    def top_copy(i):
        return remote(rho.at[MID + FAR, i + 1], out_ref.at[0, i], 2, FAR, i, 2)

    def mid_copy(i):
        return remote(
            rho.at[MID + OWN, i], rho.at[MID + PARTNER, i], 1, OWN, i, p + 1 - 2 * core
        )

    def arrival(which, i):
        return remote(
            rho.at[which, i], rho.at[which, i], 0, which, i, p + 1 - 2 * core
        )

    barrier = pltpu.get_barrier_semaphore()

    def greet(target):
        pl.semaphore_signal(
            barrier, inc=1, device_id={"na": target}, device_id_type=MESH
        )

    greet(p + 1 - 2 * core)
    greet(direct_to)

    @pl.when(is_relay)
    def _():
        greet(jnp.where(odd == 1, p - 2, p + 2))

    @pl.when(relays)
    def _():
        greet(relay_to)

    @pl.when(fed_by_relay)
    def _():
        greet(relay_from)

    for one, other in ((2, 4), (3, 4)):
        for me, peer in ((one, other), (other, one)):

            @pl.when(p == me)
            def _(peer=peer):
                greet(peer)

    pl.semaphore_wait(
        barrier,
        2
        + jnp.where(jnp.logical_or(p == 2, p == 3), 1, 0)
        + jnp.where(p == 4, 2, 0)
        + is_relay.astype(jnp.int32)
        + relays.astype(jnp.int32)
        + fed_by_relay.astype(jnp.int32),
    )

    direct_copy(0).start()
    partner_copy().start()

    @pl.loop(1, direct_count)
    def _(i):
        direct_copy(i).start()

    small = [
        pltpu.make_async_copy(source, target, small_sem.at[k])
        for k, (source, target) in enumerate(
            ((damp_in, damp_ref), (creal_in, creal_ref), (cimag_in, cimag_ref))
        )
    ]
    for k in range(3):
        small[k].start()
        operator_copy(k).start()

    own_copy().start()

    for k in range(3):
        operator_copy(k).wait()
        raw = ham_buf[k]
        high, low = split(0.5 * (raw + raw.T))
        for half in range(2):
            cols = slice((3 * half + k) * M, (3 * half + k + 1) * M)
            w_left[0:M, cols] = high
            w_left[M : 2 * M, cols] = low
            w_right[cols, 0:M] = high
            w_right[cols, M : 2 * M] = low

    for copy in small:
        copy.wait()

    for mode in range(2):
        re = jnp.full((8, M), creal_ref[mode], jnp.float32)
        im = jnp.full((8, M), cimag_ref[mode], jnp.float32)
        magnitude = jnp.sqrt(re * re + im * im)

        @pl.loop(0, N)
        def _(n):
            occupied = jnp.full((8, M), n.astype(jnp.float32), jnp.float32)
            lower = jnp.sqrt(occupied / magnitude)
            table[3 * mode, n] = jnp.sqrt((occupied + 1.0) * magnitude)
            table[3 * mode + 1, n] = lower * re
            table[3 * mode + 2, n] = lower * im

    @pl.loop(K, N)
    def _(i):
        out_ref[0, i] = jnp.zeros((2, M, M), jnp.float32)

    def build(task, own, up, down, q, n):
        alive = q + n < N - 1
        alive_scale = jnp.where(alive, 1.0, 0.0)
        up = jnp.where(alive, up, own)
        above = jnp.where(alive, n + 1, n)
        below = jnp.maximum(n - 1, 0)

        def put(block, rows, part, x, is_left):
            high, low = split(x)
            across = (2 * task + part) * M
            for half, value in ((0, high), (1, low)):
                at = (3 * half + block) * M
                if is_left:
                    x_left[at + rows : at + rows + STRIP, across : across + M] = value
                else:
                    x_right[across + rows : across + rows + STRIP, at : at + M] = value

        for rows in range(0, M, STRIP):
            strip = slice(rows, rows + STRIP)
            for part in range(2):
                value = rho[own, n, part, strip, :]
                put(0, rows, part, value, True)
                put(0, rows, part, value, False)
            for mode, occupied, (ub, us), (vb, vs) in (
                (0, q, (up, n), (down, n)),
                (1, n, (own, above), (own, below)),
            ):
                raise_w = table[3 * mode, occupied, 0:1, :] * alive_scale
                direct_w = table[3 * mode + 1, occupied, 0:1, :]
                cross_w = table[3 * mode + 2, occupied, 0:1, :]
                v_re = rho[vb, vs, 0, strip, :]
                v_im = rho[vb, vs, 1, strip, :]
                e_re = raise_w * rho[ub, us, 0, strip, :] + direct_w * v_re
                e_im = raise_w * rho[ub, us, 1, strip, :] + direct_w * v_im
                x_re = cross_w * v_im
                x_im = cross_w * v_re
                put(1 + mode, rows, 0, e_re - x_re, True)
                put(1 + mode, rows, 0, e_re + x_re, False)
                put(1 + mode, rows, 1, e_im + x_im, True)
                put(1 + mode, rows, 1, e_im - x_im, False)

    def advance(tasks):
        for task, (own, up, down, q, n, base, scale, store) in enumerate(tasks):
            build(task, own, up, down, q, n)
        wide = 2 * M * len(tasks)
        lefts = jnp.dot(
            w_left[...], x_left[:, 0:wide], preferred_element_type=jnp.float32
        )
        rights = jnp.dot(
            x_right[0:wide, :], w_right[...], preferred_element_type=jnp.float32
        )
        for task, (own, up, down, q, n, base, scale, store) in enumerate(tasks):
            damping = (
                q.astype(jnp.float32) * damp_ref[0] + n.astype(jnp.float32) * damp_ref[1]
            )
            across = slice(2 * M * task, 2 * M * (task + 1))
            left = lefts[0:M, across] + lefts[M : 2 * M, across]
            right = rights[across, 0:M] + rights[across, M : 2 * M]
            change_re = left[:, M : 2 * M] - right[M : 2 * M] - damping * rho[own, n, 0]
            change_im = right[0:M] - left[:, 0:M] - damping * rho[own, n, 1]
            store(
                rho[base, n, 0] + scale * change_re, rho[base, n, 1] + scale * change_im
            )

    up = jnp.where(first, PARTNER, NEAR)
    down = jnp.where(first, jnp.where(p == 0, OWN, NEAR), PARTNER)
    near_up = jnp.where(first, OWN, FAR)
    near_down = jnp.where(first, FAR, OWN)
    near_q = jnp.where(first, p - 1, p + 1)

    def take(i):
        @pl.when(waits_near(i))
        def _():
            arrival(NEAR, i).wait_recv()

        @pl.when(passes_near(i))
        def _():
            relay_near(i).start()

        @pl.when(waits_far(i))
        def _():
            arrival(FAR, i).wait_recv()

        @pl.when(passes_far(i))
        def _():
            relay_far(i).start()

    early = jnp.logical_and(core == 1, K - 1 > EARLY + 1)
    in_turn = jnp.where(early, K - 1, own_count)

    own_copy().wait()

    lag = jnp.where(jnp.logical_and(relays, p != 1), LAG, 1)

    @pl.loop(-1, K + lag)
    def _(i):
        j = i - lag
        ahead = jnp.logical_and(early, i == EARLY)

        top = jnp.logical_and(p == 1, i == K - 2)

        @pl.loop(0, jnp.where(top, 7, jnp.where(ahead, 4, 3)))
        def _(turn):
            kind = jnp.where(top, lax.rem(turn + 1, 7), turn)
            is_final = kind == FINAL
            is_near = kind == SIDE

            @pl.when(jnp.logical_and(is_final, jnp.logical_and(j >= 0, j < pairs)))
            def _():
                mid_copy(j).wait_recv()

            @pl.when(kind == MIDDLE)
            def _():
                @pl.when(jnp.logical_and(p == 4, i == PASS_DOWN))
                def _():
                    for k in (cut, cut + 1):
                        arrival(FAR, k).wait_recv()
                        relay_far(k).start()
                        arrival(NEAR, k).wait_recv()
                        relay_near(k).start()

                c = i + 1
                extra = jnp.where(c < one_ahead, 2, jnp.where(c < none_ahead, 1, 0))
                extra = jnp.where(jnp.logical_or(p != 1, c < cut), 0, extra)
                skip = (p == 1) & ((c == one_ahead) | (c == none_ahead))

                @pl.when(jnp.logical_not(skip))
                def _():
                    take(c + extra)

                @pl.when(jnp.logical_and(p == 1, detour(c)))
                def _():
                    arrival(NEAR, c).wait_recv()
                    arrival(FAR, c).wait_recv()

                @pl.when(c == 0)
                def _():
                    partner_copy().wait_recv()

            is_own = jnp.logical_or(kind == MIDDLE, kind == AHEAD)
            is_top = kind > TOP
            n = jnp.where(kind == FINAL, j, jnp.where(kind == SIDE, i, i + 1))
            n = jnp.where(kind == AHEAD, K - 1, n)
            n = jnp.where(kind == TOP + 1, N - 3, jnp.where(kind >= TOP, N - 4, n))
            limit = jnp.where(is_final, final_count, mid_near_count)
            limit = jnp.where(kind == MIDDLE, in_turn, limit)
            limit = jnp.where(kind == AHEAD, jnp.where(ahead, K, 0), limit)
            limit = jnp.where(kind >= TOP, N, limit)
            both = (i + 1 < in_turn) & (i >= 0) & (i < mid_near_count)
            limit = jnp.where(both & ((kind == MIDDLE) | (kind == SIDE)), 0, limit)

            @pl.when(both & (kind == MIDDLE))
            def _():
                def keep(slot, at):
                    def store(real, imag):
                        rho[slot, at, 0] = real
                        rho[slot, at, 1] = imag

                    return store

                half = 0.5 * step_size
                advance(
                    [
                        (OWN, up, down, p, n, OWN, half, keep(MID + OWN, n)),
                        (
                            NEAR,
                            near_up,
                            near_down,
                            near_q,
                            i,
                            NEAR,
                            half,
                            keep(MID + NEAR, i),
                        ),
                    ]
                )

                @pl.when(n < pairs)
                def _():
                    mid_copy(n).start()


            @pl.when(jnp.logical_and(n >= 0, n < limit))
            def _():
                shift = jnp.where(jnp.logical_or(is_final, is_top), MID, 0)
                source = jnp.where(
                    kind == TOP, FAR, jnp.where(is_near | is_top, NEAR, OWN)
                )
                above = jnp.where(is_near, near_up, up)
                above = jnp.where(kind >= TOP, FAR, above)
                below = jnp.where(is_near, near_down, down)
                below = jnp.where(kind == TOP, NEAR, jnp.where(is_top, OWN, below))
                row = jnp.where(is_near, near_q, p)
                row = jnp.where(kind == TOP, p + 2, jnp.where(is_top, p + 1, row))

                def store(real, imag):
                    @pl.when(is_final)
                    def _():
                        out_ref[0, n, 0] = real
                        out_ref[0, n, 1] = imag

                    @pl.when(jnp.logical_not(is_final))
                    def _():
                        into = MID + jnp.where(is_top, FAR, source)
                        at = jnp.where(is_top, n + 1, n)
                        rho[into, at, 0] = real
                        rho[into, at, 1] = imag

                advance(
                    [
                        (
                            shift + source,
                            shift + above,
                            shift + below,
                            row,
                            n,
                            source,
                            jnp.where(shift > 0, step_size, 0.5 * step_size),
                            store,
                        )
                    ]
                )

                @pl.when(jnp.logical_and(is_own, n < pairs))
                def _():
                    mid_copy(n).start()

                @pl.when(is_top)
                def _():
                    top_copy(n).start()

    @pl.when(p == 2)
    def _():
        for i in range(N - 4, N - 2):
            top_copy(i).wait_recv()

    partner_copy().wait_send()

    aside = jnp.where(p == 4, 2, 0)
    sends = (
        direct_count,
        pairs,
        relay_near_count + aside,
        relay_far_count + aside - jnp.where(p == 1, 2, 0),
    )
    for row, count in enumerate(sends):
        for k in range(1, N + 1):

            @pl.when(count == k)
            def _(row=row, k=k):
                pltpu.make_async_remote_copy(
                    src_ref=rho.at[OWN, 0:k],
                    dst_ref=rho.at[OWN, 0:k],
                    send_sem=send_sem.at[row],
                    recv_sem=recv_sem.at[0, 0],
                    device_id={"na": p + 1 - 2 * core},
                    device_id_type=MESH,
                ).wait_send()


def per_device(hierarchy, hamiltonian, couplings, damp_rates, coef_real, coef_imag):
    total = hierarchy.shape[1]
    M = hierarchy.shape[-1]
    hbm = pl.BlockSpec(memory_space=pltpu.HBM)
    return pl.pallas_call(
        functools.partial(kernel, total, M),
        out_shape=pltpu.VMEM(hierarchy.shape, jnp.float32),
        in_specs=[hbm] * 6,
        out_specs=pl.BlockSpec(memory_space=pltpu.VMEM),
        scratch_shapes=[
            pltpu.VMEM((MID + 4, total, 2, M, M), jnp.float32),
            pltpu.VMEM((2 * M, 6 * M), jnp.bfloat16),
            pltpu.VMEM((6 * M, 2 * M), jnp.bfloat16),
            pltpu.VMEM((6 * M, 4 * M), jnp.bfloat16),
            pltpu.VMEM((4 * M, 6 * M), jnp.bfloat16),
            pltpu.VMEM((6, total, 8, M), jnp.float32),
            pltpu.VMEM((3, M, M), jnp.float32),
            pltpu.SMEM(damp_rates.shape, jnp.float32),
            pltpu.SMEM(coef_real.shape, jnp.float32),
            pltpu.SMEM(coef_imag.shape, jnp.float32),
            pltpu.SemaphoreType.DMA((3,)),
            pltpu.SemaphoreType.DMA((3,)),
            pltpu.SemaphoreType.DMA((3,)),
            pltpu.SemaphoreType.DMA((4,)),
            pltpu.SemaphoreType.DMA((3, total)),
        ],
        compiler_params=pltpu.CompilerParams(
            collective_id=0, has_side_effects=True, vmem_limit_bytes=(8 + total) * 2**20
        ),
    )(
        *(
            pltpu.with_memory_space_constraint(x, pltpu.HBM)
            for x in (
                hierarchy,
                hamiltonian,
                couplings,
                damp_rates,
                coef_real,
                coef_imag,
            )
        )
    )


def solution(mesh):
    in_specs = (
        P(("sweep", "na"), None, None, None, None),
        P(),
        P(),
        P("sweep"),
        P("sweep"),
        P("sweep"),
    )
    out_specs = P(("sweep", "na"), None, None, None, None)
    return jax.shard_map(
        per_device, mesh=mesh, in_specs=in_specs, out_specs=out_specs, check_vma=False
    )
```

```python
import functools
import jax
import jax.numpy as jnp
from jax import lax
from jax.experimental import pallas as pl
from jax.experimental.pallas import tpu as pltpu
from jax.sharding import PartitionSpec as P

step_size = 0.02
MESH = pl.DeviceIdType.MESH
NEAR, OWN, PARTNER, FAR, MID = 0, 1, 2, 3, 4
STRIP = 32
LAG = 2
EARLY = 3
PASS_DOWN = 1
FINAL, MIDDLE, SIDE, AHEAD, TOP = 0, 1, 2, 3, 4


def split(x):
    high = x.astype(jnp.bfloat16)
    return high, (x - high.astype(jnp.float32)).astype(jnp.bfloat16)


def kernel(
    total,
    order,
    hier_ref,
    ham_ref,
    coup_ref,
    damp_in,
    creal_in,
    cimag_in,
    out_ref,
    rho,
    w_left,
    w_right,
    x_left,
    x_right,
    table,
    ham_buf,
    damp_ref,
    creal_ref,
    cimag_ref,
    own_sem,
    ham_sem,
    small_sem,
    send_sem,
    recv_sem,
):
    M, N = order, total
    p = lax.axis_index("na")
    chip = p // 2
    core = p % 2
    odd = chip % 2
    chips = N // 2
    first = core == 0
    K = N - p
    pairs = N - 1 - 2 * chip

    is_relay = core != odd
    relays = jnp.logical_and(
        is_relay, jnp.where(odd == 1, chip >= 2, chip + 2 < chips)
    )
    fed_by_relay = jnp.logical_and(
        core == odd, jnp.where(odd == 1, chip + 2 < chips, chip >= 2)
    )
    direct_to = jnp.where(odd == 1, 2 * chip - 1, 2 * chip + 2)
    relay_to = jnp.where(odd == 1, p - 3, p + 3)
    relay_from = jnp.where(odd == 1, p + 3, p - 3)

    direct_count = jnp.where(p == 0, K - 4, jnp.where(p == 1, K - 2, K))
    near_count = jnp.where(first, jnp.where(p == 0, 0, K + 1), K - 1)
    near_count = jnp.where(p == 2, K - 1, near_count)
    far_count = jnp.where(
        first,
        jnp.where(
            p == 0, 0, jnp.where(jnp.logical_and(odd == 1, chip >= 2), K + 2, K)
        ),
        jnp.maximum(K - 2, 0),
    )
    far_count = jnp.where(p == 2, K - 2, far_count)
    relay_near_count = jnp.where(relays, jnp.where(first, near_count, K - 3), 0)
    relay_far_count = jnp.where(relays, far_count, 0)
    mid_near_count = jnp.where(first, jnp.where(p == 0, 0, K), K - 1)
    mid_near_count = jnp.where(p == 2, K - 2, mid_near_count)
    own_count = jnp.where(p == 2, K - 1, K)
    final_count = jnp.where(p == 2, K - 2, K)
    direct_slot = jnp.where(core == odd, FAR, NEAR)

    cut = N // 3
    one_ahead = N // 2
    none_ahead = N - 5

    def detour(i):
        return jnp.logical_and(i >= cut, i < cut + 2)

    def via_upper(i):
        return jnp.logical_and((p == 2) | (p == 3), detour(i))

    def direct_target(i):
        return jnp.where(via_upper(i), 4, direct_to)

    def elsewhere(i):
        return jnp.logical_and((p == 1) | (p == 4), detour(i))

    def waits_near(i):
        return jnp.logical_and(i < near_count, jnp.logical_not(elsewhere(i)))

    def waits_far(i):
        return jnp.logical_and(i < far_count, jnp.logical_not(elsewhere(i)))

    def passes_near(i):
        return jnp.logical_and(i < relay_near_count, jnp.logical_not(elsewhere(i)))

    def passes_far(i):
        return jnp.logical_and(i < relay_far_count, jnp.logical_not(elsewhere(i)))

    relay_to = jnp.where(p == 4, 1, relay_to)

    def own_copy():
        return pltpu.make_async_copy(hier_ref.at[0], rho.at[OWN], own_sem.at[0])

    def operator_copy(k):
        return pltpu.make_async_copy(
            ham_ref if k == 0 else coup_ref.at[k - 1], ham_buf.at[k], ham_sem.at[k]
        )

    def remote(src, dst, send, recv, i, target):
        return pltpu.make_async_remote_copy(
            src_ref=src,
            dst_ref=dst,
            send_sem=send_sem.at[send],
            recv_sem=recv_sem.at[recv - recv // 3, i],
            device_id={"na": target},
            device_id_type=MESH,
        )

    def direct_copy(i):
        slot = jnp.where(via_upper(i), NEAR + FAR - direct_slot, direct_slot)
        return remote(
            hier_ref.at[0, i], rho.at[slot, i], 0, slot, i, direct_target(i)
        )

    def partner_copy():
        return pltpu.make_async_remote_copy(
            src_ref=hier_ref.at[0],
            dst_ref=rho.at[PARTNER],
            send_sem=own_sem.at[1],
            recv_sem=own_sem.at[2],
            device_id={"na": p + 1 - 2 * core},
            device_id_type=MESH,
        )

    def relay_near(i):
        return remote(rho.at[NEAR, i], rho.at[FAR, i], 2, FAR, i, relay_to)

    def relay_far(i):
        return remote(rho.at[FAR, i], rho.at[NEAR, i], 3, NEAR, i, relay_to)

    def top_copy(i):
        return remote(rho.at[MID + FAR, i + 1], out_ref.at[0, i], 2, FAR, i, 2)

    def mid_copy(i):
        return remote(
            rho.at[MID + OWN, i], rho.at[MID + PARTNER, i], 1, OWN, i, p + 1 - 2 * core
        )

    def arrival(which, i):
        return remote(
            rho.at[which, i], rho.at[which, i], 0, which, i, p + 1 - 2 * core
        )

    barrier = pltpu.get_barrier_semaphore()

    def greet(target):
        pl.semaphore_signal(
            barrier, inc=1, device_id={"na": target}, device_id_type=MESH
        )

    greet(p + 1 - 2 * core)
    greet(direct_to)

    @pl.when(is_relay)
    def _():
        greet(jnp.where(odd == 1, p - 2, p + 2))

    @pl.when(relays)
    def _():
        greet(relay_to)

    @pl.when(fed_by_relay)
    def _():
        greet(relay_from)

    for one, other in ((2, 4), (3, 4)):
        for me, peer in ((one, other), (other, one)):

            @pl.when(p == me)
            def _(peer=peer):
                greet(peer)

    pl.semaphore_wait(
        barrier,
        2
        + jnp.where(jnp.logical_or(p == 2, p == 3), 1, 0)
        + jnp.where(p == 4, 2, 0)
        + is_relay.astype(jnp.int32)
        + relays.astype(jnp.int32)
        + fed_by_relay.astype(jnp.int32),
    )

    direct_copy(0).start()
    partner_copy().start()

    @pl.loop(1, direct_count)
    def _(i):
        direct_copy(i).start()

    small = [
        pltpu.make_async_copy(source, target, small_sem.at[k])
        for k, (source, target) in enumerate(
            ((damp_in, damp_ref), (creal_in, creal_ref), (cimag_in, cimag_ref))
        )
    ]
    for k in range(3):
        small[k].start()
        operator_copy(k).start()

    own_copy().start()

    for k in range(3):
        operator_copy(k).wait()
        raw = ham_buf[k]
        high, low = split(0.5 * (raw + raw.T))
        for half in range(2):
            cols = slice((3 * half + k) * M, (3 * half + k + 1) * M)
            w_left[0:M, cols] = high
            w_left[M : 2 * M, cols] = low
            w_right[cols, 0:M] = high
            w_right[cols, M : 2 * M] = low

    for copy in small:
        copy.wait()

    for mode in range(2):
        re = jnp.full((8, M), creal_ref[mode], jnp.float32)
        im = jnp.full((8, M), cimag_ref[mode], jnp.float32)
        magnitude = jnp.sqrt(re * re + im * im)

        @pl.loop(0, N)
        def _(n):
            occupied = jnp.full((8, M), n.astype(jnp.float32), jnp.float32)
            lower = jnp.sqrt(occupied / magnitude)
            table[3 * mode, n] = jnp.sqrt((occupied + 1.0) * magnitude)
            table[3 * mode + 1, n] = lower * re
            table[3 * mode + 2, n] = lower * im

    @pl.loop(K, N)
    def _(i):
        out_ref[0, i] = jnp.zeros((2, M, M), jnp.float32)

    def build(task, own, up, down, q, n):
        alive = q + n < N - 1
        alive_scale = jnp.where(alive, 1.0, 0.0)
        up = jnp.where(alive, up, own)
        above = jnp.where(alive, n + 1, n)
        below = jnp.maximum(n - 1, 0)

        def put(block, rows, part, x, is_left):
            high, low = split(x)
            across = (2 * task + part) * M
            for half, value in ((0, high), (1, low)):
                at = (3 * half + block) * M
                if is_left:
                    x_left[at + rows : at + rows + STRIP, across : across + M] = value
                else:
                    x_right[across + rows : across + rows + STRIP, at : at + M] = value

        for rows in range(0, M, STRIP):
            strip = slice(rows, rows + STRIP)
            for part in range(2):
                value = rho[own, n, part, strip, :]
                put(0, rows, part, value, True)
                put(0, rows, part, value, False)
            for mode, occupied, (ub, us), (vb, vs) in (
                (0, q, (up, n), (down, n)),
                (1, n, (own, above), (own, below)),
            ):
                raise_w = table[3 * mode, occupied, 0:1, :] * alive_scale
                direct_w = table[3 * mode + 1, occupied, 0:1, :]
                cross_w = table[3 * mode + 2, occupied, 0:1, :]
                v_re = rho[vb, vs, 0, strip, :]
                v_im = rho[vb, vs, 1, strip, :]
                e_re = raise_w * rho[ub, us, 0, strip, :] + direct_w * v_re
                e_im = raise_w * rho[ub, us, 1, strip, :] + direct_w * v_im
                x_re = cross_w * v_im
                x_im = cross_w * v_re
                put(1 + mode, rows, 0, e_re - x_re, True)
                put(1 + mode, rows, 0, e_re + x_re, False)
                put(1 + mode, rows, 1, e_im + x_im, True)
                put(1 + mode, rows, 1, e_im - x_im, False)

    def advance(tasks):
        for task, (own, up, down, q, n, base, scale, store) in enumerate(tasks):
            build(task, own, up, down, q, n)
        wide = 2 * M * len(tasks)
        lefts = jnp.dot(
            w_left[...], x_left[:, 0:wide], preferred_element_type=jnp.float32
        )
        rights = jnp.dot(
            x_right[0:wide, :], w_right[...], preferred_element_type=jnp.float32
        )
        for task, (own, up, down, q, n, base, scale, store) in enumerate(tasks):
            damping = (
                q.astype(jnp.float32) * damp_ref[0] + n.astype(jnp.float32) * damp_ref[1]
            )
            across = slice(2 * M * task, 2 * M * (task + 1))
            left = lefts[0:M, across] + lefts[M : 2 * M, across]
            right = rights[across, 0:M] + rights[across, M : 2 * M]
            change_re = left[:, M : 2 * M] - right[M : 2 * M] - damping * rho[own, n, 0]
            change_im = right[0:M] - left[:, 0:M] - damping * rho[own, n, 1]
            store(
                rho[base, n, 0] + scale * change_re, rho[base, n, 1] + scale * change_im
            )

    up = jnp.where(first, PARTNER, NEAR)
    down = jnp.where(first, jnp.where(p == 0, OWN, NEAR), PARTNER)
    near_up = jnp.where(first, OWN, FAR)
    near_down = jnp.where(first, FAR, OWN)
    near_q = jnp.where(first, p - 1, p + 1)

    def take(i):
        @pl.when(waits_near(i))
        def _():
            arrival(NEAR, i).wait_recv()

        @pl.when(passes_near(i))
        def _():
            relay_near(i).start()

        @pl.when(waits_far(i))
        def _():
            arrival(FAR, i).wait_recv()

        @pl.when(passes_far(i))
        def _():
            relay_far(i).start()

    early = jnp.logical_and(core == 1, K - 1 > EARLY + 1)
    in_turn = jnp.where(early, K - 1, own_count)

    own_copy().wait()

    lag = jnp.where(jnp.logical_and(relays, p != 1), LAG, 1)

    @pl.loop(-1, K + lag)
    def _(i):
        j = i - lag
        ahead = jnp.logical_and(early, i == EARLY)

        top = jnp.logical_and(p == 1, i == K - 2)

        @pl.loop(0, jnp.where(top, 7, jnp.where(ahead, 4, 3)))
        def _(turn):
            kind = jnp.where(top, lax.rem(turn + 1, 7), turn)
            is_final = kind == FINAL
            is_near = kind == SIDE

            @pl.when(jnp.logical_and(is_final, jnp.logical_and(j >= 0, j < pairs)))
            def _():
                mid_copy(j).wait_recv()

            @pl.when(kind == MIDDLE)
            def _():
                @pl.when(jnp.logical_and(p == 4, i == PASS_DOWN))
                def _():
                    for k in (cut, cut + 1):
                        arrival(FAR, k).wait_recv()
                        relay_far(k).start()
                        arrival(NEAR, k).wait_recv()
                        relay_near(k).start()

                c = i + 1
                extra = jnp.where(c < one_ahead, 2, jnp.where(c < none_ahead, 1, 0))
                extra = jnp.where(jnp.logical_or(p != 1, c < cut), 0, extra)
                skip = (p == 1) & ((c == one_ahead) | (c == none_ahead))

                @pl.when(jnp.logical_not(skip))
                def _():
                    take(c + extra)

                @pl.when(jnp.logical_and(p == 1, detour(c)))
                def _():
                    arrival(NEAR, c).wait_recv()
                    arrival(FAR, c).wait_recv()

                @pl.when(c == 0)
                def _():
                    partner_copy().wait_recv()

            is_own = jnp.logical_or(kind == MIDDLE, kind == AHEAD)
            is_top = kind > TOP
            n = jnp.where(kind == FINAL, j, jnp.where(kind == SIDE, i, i + 1))
            n = jnp.where(kind == AHEAD, K - 1, n)
            n = jnp.where(kind == TOP + 1, N - 3, jnp.where(kind >= TOP, N - 4, n))
            limit = jnp.where(is_final, final_count, mid_near_count)
            limit = jnp.where(kind == MIDDLE, in_turn, limit)
            limit = jnp.where(kind == AHEAD, jnp.where(ahead, K, 0), limit)
            limit = jnp.where(kind >= TOP, N, limit)
            both = (i + 1 < in_turn) & (i >= 0) & (i < mid_near_count)
            limit = jnp.where(both & ((kind == MIDDLE) | (kind == SIDE)), 0, limit)

            @pl.when(both & (kind == MIDDLE))
            def _():
                def keep(slot, at):
                    def store(real, imag):
                        rho[slot, at, 0] = real
                        rho[slot, at, 1] = imag

                    return store

                half = 0.5 * step_size
                advance(
                    [
                        (OWN, up, down, p, n, OWN, half, keep(MID + OWN, n)),
                        (
                            NEAR,
                            near_up,
                            near_down,
                            near_q,
                            i,
                            NEAR,
                            half,
                            keep(MID + NEAR, i),
                        ),
                    ]
                )

                @pl.when(n < pairs)
                def _():
                    mid_copy(n).start()


            @pl.when(jnp.logical_and(n >= 0, n < limit))
            def _():
                shift = jnp.where(jnp.logical_or(is_final, is_top), MID, 0)
                source = jnp.where(
                    kind == TOP, FAR, jnp.where(is_near | is_top, NEAR, OWN)
                )
                above = jnp.where(is_near, near_up, up)
                above = jnp.where(kind >= TOP, FAR, above)
                below = jnp.where(is_near, near_down, down)
                below = jnp.where(kind == TOP, NEAR, jnp.where(is_top, OWN, below))
                row = jnp.where(is_near, near_q, p)
                row = jnp.where(kind == TOP, p + 2, jnp.where(is_top, p + 1, row))

                def store(real, imag):
                    @pl.when(is_final)
                    def _():
                        out_ref[0, n, 0] = real
                        out_ref[0, n, 1] = imag

                    @pl.when(jnp.logical_not(is_final))
                    def _():
                        into = MID + jnp.where(is_top, FAR, source)
                        at = jnp.where(is_top, n + 1, n)
                        rho[into, at, 0] = real
                        rho[into, at, 1] = imag

                advance(
                    [
                        (
                            shift + source,
                            shift + above,
                            shift + below,
                            row,
                            n,
                            source,
                            jnp.where(shift > 0, step_size, 0.5 * step_size),
                            store,
                        )
                    ]
                )

                @pl.when(jnp.logical_and(is_own, n < pairs))
                def _():
                    mid_copy(n).start()

                @pl.when(is_top)
                def _():
                    top_copy(n).start()

    @pl.when(p == 2)
    def _():
        for i in range(N - 4, N - 2):
            top_copy(i).wait_recv()

    partner_copy().wait_send()

    aside = jnp.where(p == 4, 2, 0)
    sends = (
        direct_count,
        pairs,
        relay_near_count + aside,
        relay_far_count + aside - jnp.where(p == 1, 2, 0),
    )

    def settle(row, count, low, high):
        if high - low > 1:
            middle = (low + high) // 2

            @pl.when(count < middle)
            def _():
                settle(row, count, low, middle)

            @pl.when(count >= middle)
            def _():
                settle(row, count, middle, high)

        elif low > 0:
            pltpu.make_async_remote_copy(
                src_ref=rho.at[OWN, 0:low],
                dst_ref=rho.at[OWN, 0:low],
                send_sem=send_sem.at[row],
                recv_sem=recv_sem.at[0, 0],
                device_id={"na": p + 1 - 2 * core},
                device_id_type=MESH,
            ).wait_send()

    for row, count in enumerate(sends):
        settle(row, count, 0, N + 1)


def per_device(hierarchy, hamiltonian, couplings, damp_rates, coef_real, coef_imag):
    total = hierarchy.shape[1]
    M = hierarchy.shape[-1]
    hbm = pl.BlockSpec(memory_space=pltpu.HBM)
    return pl.pallas_call(
        functools.partial(kernel, total, M),
        out_shape=pltpu.VMEM(hierarchy.shape, jnp.float32),
        in_specs=[hbm] * 6,
        out_specs=pl.BlockSpec(memory_space=pltpu.VMEM),
        scratch_shapes=[
            pltpu.VMEM((MID + 4, total, 2, M, M), jnp.float32),
            pltpu.VMEM((2 * M, 6 * M), jnp.bfloat16),
            pltpu.VMEM((6 * M, 2 * M), jnp.bfloat16),
            pltpu.VMEM((6 * M, 4 * M), jnp.bfloat16),
            pltpu.VMEM((4 * M, 6 * M), jnp.bfloat16),
            pltpu.VMEM((6, total, 8, M), jnp.float32),
            pltpu.VMEM((3, M, M), jnp.float32),
            pltpu.SMEM(damp_rates.shape, jnp.float32),
            pltpu.SMEM(coef_real.shape, jnp.float32),
            pltpu.SMEM(coef_imag.shape, jnp.float32),
            pltpu.SemaphoreType.DMA((3,)),
            pltpu.SemaphoreType.DMA((3,)),
            pltpu.SemaphoreType.DMA((3,)),
            pltpu.SemaphoreType.DMA((4,)),
            pltpu.SemaphoreType.DMA((3, total)),
        ],
        compiler_params=pltpu.CompilerParams(
            collective_id=0, has_side_effects=True, vmem_limit_bytes=(8 + total) * 2**20
        ),
    )(
        *(
            pltpu.with_memory_space_constraint(x, pltpu.HBM)
            for x in (
                hierarchy,
                hamiltonian,
                couplings,
                damp_rates,
                coef_real,
                coef_imag,
            )
        )
    )


def solution(mesh):
    in_specs = (
        P(("sweep", "na"), None, None, None, None),
        P(),
        P(),
        P("sweep"),
        P("sweep"),
        P("sweep"),
    )
    out_specs = P(("sweep", "na"), None, None, None, None)
    return jax.shard_map(
        per_device, mesh=mesh, in_specs=in_specs, out_specs=out_specs, check_vma=False
    )
```

```python
import functools
import jax
import jax.numpy as jnp
from jax import lax
from jax.experimental import pallas as pl
from jax.experimental.pallas import tpu as pltpu
from jax.sharding import PartitionSpec as P

step_size = 0.02
MESH = pl.DeviceIdType.MESH
NEAR, OWN, PARTNER, FAR, MID = 0, 1, 2, 3, 4
STRIP = 32
LAG = 2
EARLY = 3
PASS_DOWN = 1
FINAL, MIDDLE, SIDE, AHEAD, TOP = 0, 1, 2, 3, 4


def split(x):
    high = x.astype(jnp.bfloat16)
    return high, (x - high.astype(jnp.float32)).astype(jnp.bfloat16)


def kernel(
    total,
    order,
    hier_ref,
    ham_ref,
    coup_ref,
    damp_in,
    creal_in,
    cimag_in,
    out_ref,
    rho,
    w_left,
    w_right,
    x_left,
    x_right,
    table,
    ham_buf,
    damp_ref,
    creal_ref,
    cimag_ref,
    own_sem,
    ham_sem,
    small_sem,
    send_sem,
    recv_sem,
):
    M, N = order, total
    p = lax.axis_index("na")
    chip = p // 2
    core = p % 2
    odd = chip % 2
    chips = N // 2
    first = core == 0
    K = N - p
    pairs = N - 1 - 2 * chip

    is_relay = core != odd
    relays = jnp.logical_and(
        is_relay, jnp.where(odd == 1, chip >= 2, chip + 2 < chips)
    )
    fed_by_relay = jnp.logical_and(
        core == odd, jnp.where(odd == 1, chip + 2 < chips, chip >= 2)
    )
    direct_to = jnp.where(odd == 1, 2 * chip - 1, 2 * chip + 2)
    relay_to = jnp.where(odd == 1, p - 3, p + 3)
    relay_from = jnp.where(odd == 1, p + 3, p - 3)

    direct_count = jnp.where(p == 0, K - 4, jnp.where(p == 1, K - 2, K))
    near_count = jnp.where(first, jnp.where(p == 0, 0, K + 1), K - 1)
    near_count = jnp.where(p == 2, K - 1, near_count)
    far_count = jnp.where(
        first,
        jnp.where(
            p == 0, 0, jnp.where(jnp.logical_and(odd == 1, chip >= 2), K + 2, K)
        ),
        jnp.maximum(K - 2, 0),
    )
    far_count = jnp.where(p == 2, K - 2, far_count)
    relay_near_count = jnp.where(relays, jnp.where(first, near_count, K - 3), 0)
    relay_far_count = jnp.where(relays, far_count, 0)
    mid_near_count = jnp.where(first, jnp.where(p == 0, 0, K), K - 1)
    mid_near_count = jnp.where(p == 2, K - 2, mid_near_count)
    own_count = jnp.where(p == 2, K - 1, K)
    final_count = jnp.where(p == 2, K - 2, K)
    direct_slot = jnp.where(core == odd, FAR, NEAR)

    cut = N // 3
    one_ahead = N // 2
    none_ahead = N - 5

    def detour(i):
        return jnp.logical_and(i >= cut, i < cut + 2)

    def via_upper(i):
        return jnp.logical_and((p == 2) | (p == 3), detour(i))

    def direct_target(i):
        return jnp.where(via_upper(i), 4, direct_to)

    def elsewhere(i):
        return jnp.logical_and((p == 1) | (p == 4), detour(i))

    def waits_near(i):
        return jnp.logical_and(i < near_count, jnp.logical_not(elsewhere(i)))

    def waits_far(i):
        return jnp.logical_and(i < far_count, jnp.logical_not(elsewhere(i)))

    def passes_near(i):
        return jnp.logical_and(i < relay_near_count, jnp.logical_not(elsewhere(i)))

    def passes_far(i):
        return jnp.logical_and(i < relay_far_count, jnp.logical_not(elsewhere(i)))

    relay_to = jnp.where(p == 4, 1, relay_to)

    def own_copy():
        return pltpu.make_async_copy(hier_ref.at[0], rho.at[OWN], own_sem.at[0])

    def operator_copy(k):
        return pltpu.make_async_copy(
            ham_ref if k == 0 else coup_ref.at[k - 1], ham_buf.at[k], ham_sem.at[k]
        )

    def remote(src, dst, send, recv, i, target):
        return pltpu.make_async_remote_copy(
            src_ref=src,
            dst_ref=dst,
            send_sem=send_sem.at[send],
            recv_sem=recv_sem.at[recv - recv // 3, i],
            device_id={"na": target},
            device_id_type=MESH,
        )

    def direct_copy(i):
        slot = jnp.where(via_upper(i), NEAR + FAR - direct_slot, direct_slot)
        return remote(
            hier_ref.at[0, i], rho.at[slot, i], 0, slot, i, direct_target(i)
        )

    def partner_copy():
        return pltpu.make_async_remote_copy(
            src_ref=hier_ref.at[0],
            dst_ref=rho.at[PARTNER],
            send_sem=own_sem.at[1],
            recv_sem=own_sem.at[2],
            device_id={"na": p + 1 - 2 * core},
            device_id_type=MESH,
        )

    def relay_near(i):
        return remote(rho.at[NEAR, i], rho.at[FAR, i], 2, FAR, i, relay_to)

    def relay_far(i):
        return remote(rho.at[FAR, i], rho.at[NEAR, i], 3, NEAR, i, relay_to)

    def top_copy(i):
        return remote(rho.at[MID + FAR, i + 1], out_ref.at[0, i], 2, FAR, i, 2)

    def mid_copy(i):
        return remote(
            rho.at[MID + OWN, i], rho.at[MID + PARTNER, i], 1, OWN, i, p + 1 - 2 * core
        )

    def arrival(which, i):
        return remote(
            rho.at[which, i], rho.at[which, i], 0, which, i, p + 1 - 2 * core
        )

    barrier = pltpu.get_barrier_semaphore()

    def greet(target):
        pl.semaphore_signal(
            barrier, inc=1, device_id={"na": target}, device_id_type=MESH
        )

    greet(p + 1 - 2 * core)
    greet(direct_to)

    @pl.when(is_relay)
    def _():
        greet(jnp.where(odd == 1, p - 2, p + 2))

    @pl.when(relays)
    def _():
        greet(relay_to)

    @pl.when(fed_by_relay)
    def _():
        greet(relay_from)

    for one, other in ((2, 4), (3, 4)):
        for me, peer in ((one, other), (other, one)):

            @pl.when(p == me)
            def _(peer=peer):
                greet(peer)

    pl.semaphore_wait(
        barrier,
        2
        + jnp.where(jnp.logical_or(p == 2, p == 3), 1, 0)
        + jnp.where(p == 4, 2, 0)
        + is_relay.astype(jnp.int32)
        + relays.astype(jnp.int32)
        + fed_by_relay.astype(jnp.int32),
    )

    @pl.loop(0, direct_count)
    def _(i):
        direct_copy(i).start()

    partner_copy().start()

    small = [
        pltpu.make_async_copy(source, target, small_sem.at[k])
        for k, (source, target) in enumerate(
            ((damp_in, damp_ref), (creal_in, creal_ref), (cimag_in, cimag_ref))
        )
    ]
    for k in range(3):
        small[k].start()
        operator_copy(k).start()

    own_copy().start()

    for k in range(3):
        operator_copy(k).wait()
        raw = ham_buf[k]
        high, low = split(0.5 * (raw + raw.T))
        for half in range(2):
            cols = slice((3 * half + k) * M, (3 * half + k + 1) * M)
            w_left[0:M, cols] = high
            w_left[M : 2 * M, cols] = low
            w_right[cols, 0:M] = high
            w_right[cols, M : 2 * M] = low

    for copy in small:
        copy.wait()

    for mode in range(2):
        re = jnp.full((8, M), creal_ref[mode], jnp.float32)
        im = jnp.full((8, M), cimag_ref[mode], jnp.float32)
        magnitude = jnp.sqrt(re * re + im * im)

        @pl.loop(0, N)
        def _(n):
            occupied = jnp.full((8, M), n.astype(jnp.float32), jnp.float32)
            lower = jnp.sqrt(occupied / magnitude)
            table[3 * mode, n] = jnp.sqrt((occupied + 1.0) * magnitude)
            table[3 * mode + 1, n] = lower * re
            table[3 * mode + 2, n] = lower * im

    @pl.loop(K, N)
    def _(i):
        out_ref[0, i] = jnp.zeros((2, M, M), jnp.float32)

    def build(task, own, up, down, q, n):
        alive = q + n < N - 1
        alive_scale = jnp.where(alive, 1.0, 0.0)
        up = jnp.where(alive, up, own)
        above = jnp.where(alive, n + 1, n)
        below = jnp.maximum(n - 1, 0)

        def put(block, rows, part, x, is_left):
            high, low = split(x)
            across = (2 * task + part) * M
            for half, value in ((0, high), (1, low)):
                at = (3 * half + block) * M
                if is_left:
                    x_left[at + rows : at + rows + STRIP, across : across + M] = value
                else:
                    x_right[across + rows : across + rows + STRIP, at : at + M] = value

        for rows in range(0, M, STRIP):
            strip = slice(rows, rows + STRIP)
            for part in range(2):
                value = rho[own, n, part, strip, :]
                put(0, rows, part, value, True)
                put(0, rows, part, value, False)
            for mode, occupied, (ub, us), (vb, vs) in (
                (0, q, (up, n), (down, n)),
                (1, n, (own, above), (own, below)),
            ):
                raise_w = table[3 * mode, occupied, 0:1, :] * alive_scale
                direct_w = table[3 * mode + 1, occupied, 0:1, :]
                cross_w = table[3 * mode + 2, occupied, 0:1, :]
                v_re = rho[vb, vs, 0, strip, :]
                v_im = rho[vb, vs, 1, strip, :]
                e_re = raise_w * rho[ub, us, 0, strip, :] + direct_w * v_re
                e_im = raise_w * rho[ub, us, 1, strip, :] + direct_w * v_im
                x_re = cross_w * v_im
                x_im = cross_w * v_re
                put(1 + mode, rows, 0, e_re - x_re, True)
                put(1 + mode, rows, 0, e_re + x_re, False)
                put(1 + mode, rows, 1, e_im + x_im, True)
                put(1 + mode, rows, 1, e_im - x_im, False)

    def advance(tasks):
        for task, (own, up, down, q, n, base, scale, store) in enumerate(tasks):
            build(task, own, up, down, q, n)
        wide = 2 * M * len(tasks)
        lefts = jnp.dot(
            w_left[...], x_left[:, 0:wide], preferred_element_type=jnp.float32
        )
        rights = jnp.dot(
            x_right[0:wide, :], w_right[...], preferred_element_type=jnp.float32
        )
        for task, (own, up, down, q, n, base, scale, store) in enumerate(tasks):
            damping = (
                q.astype(jnp.float32) * damp_ref[0] + n.astype(jnp.float32) * damp_ref[1]
            )
            across = slice(2 * M * task, 2 * M * (task + 1))
            left = lefts[0:M, across] + lefts[M : 2 * M, across]
            right = rights[across, 0:M] + rights[across, M : 2 * M]
            change_re = left[:, M : 2 * M] - right[M : 2 * M] - damping * rho[own, n, 0]
            change_im = right[0:M] - left[:, 0:M] - damping * rho[own, n, 1]
            store(
                rho[base, n, 0] + scale * change_re, rho[base, n, 1] + scale * change_im
            )

    up = jnp.where(first, PARTNER, NEAR)
    down = jnp.where(first, jnp.where(p == 0, OWN, NEAR), PARTNER)
    near_up = jnp.where(first, OWN, FAR)
    near_down = jnp.where(first, FAR, OWN)
    near_q = jnp.where(first, p - 1, p + 1)

    def take(i):
        @pl.when(waits_near(i))
        def _():
            arrival(NEAR, i).wait_recv()

        @pl.when(passes_near(i))
        def _():
            relay_near(i).start()

        @pl.when(waits_far(i))
        def _():
            arrival(FAR, i).wait_recv()

        @pl.when(passes_far(i))
        def _():
            relay_far(i).start()

    early = jnp.logical_and(core == 1, K - 1 > EARLY + 1)
    in_turn = jnp.where(early, K - 1, own_count)

    own_copy().wait()

    lag = jnp.where(jnp.logical_and(relays, p != 1), LAG, 1)

    @pl.loop(-1, K + lag)
    def _(i):
        j = i - lag
        ahead = jnp.logical_and(early, i == EARLY)

        top = jnp.logical_and(p == 1, i == K - 2)

        @pl.loop(0, jnp.where(top, 7, jnp.where(ahead, 4, 3)))
        def _(turn):
            kind = jnp.where(top, lax.rem(turn + 1, 7), turn)
            is_final = kind == FINAL
            is_near = kind == SIDE

            @pl.when(jnp.logical_and(is_final, jnp.logical_and(j >= 0, j < pairs)))
            def _():
                mid_copy(j).wait_recv()

            @pl.when(kind == MIDDLE)
            def _():
                @pl.when(jnp.logical_and(p == 4, i == PASS_DOWN))
                def _():
                    for k in (cut, cut + 1):
                        arrival(FAR, k).wait_recv()
                        relay_far(k).start()
                        arrival(NEAR, k).wait_recv()
                        relay_near(k).start()

                c = i + 1
                extra = jnp.where(c < one_ahead, 2, jnp.where(c < none_ahead, 1, 0))
                extra = jnp.where(jnp.logical_or(p != 1, c < cut), 0, extra)
                skip = (p == 1) & ((c == one_ahead) | (c == none_ahead))

                @pl.when(jnp.logical_not(skip))
                def _():
                    take(c + extra)

                @pl.when(jnp.logical_and(p == 1, detour(c)))
                def _():
                    arrival(NEAR, c).wait_recv()
                    arrival(FAR, c).wait_recv()

                @pl.when(c == 0)
                def _():
                    partner_copy().wait_recv()

            is_own = jnp.logical_or(kind == MIDDLE, kind == AHEAD)
            is_top = kind > TOP
            n = jnp.where(kind == FINAL, j, jnp.where(kind == SIDE, i, i + 1))
            n = jnp.where(kind == AHEAD, K - 1, n)
            n = jnp.where(kind == TOP + 1, N - 3, jnp.where(kind >= TOP, N - 4, n))
            limit = jnp.where(is_final, final_count, mid_near_count)
            limit = jnp.where(kind == MIDDLE, in_turn, limit)
            limit = jnp.where(kind == AHEAD, jnp.where(ahead, K, 0), limit)
            limit = jnp.where(kind >= TOP, N, limit)
            both = (i + 1 < in_turn) & (i >= 0) & (i < mid_near_count)
            limit = jnp.where(both & ((kind == MIDDLE) | (kind == SIDE)), 0, limit)

            @pl.when(both & (kind == MIDDLE))
            def _():
                def keep(slot, at):
                    def store(real, imag):
                        rho[slot, at, 0] = real
                        rho[slot, at, 1] = imag

                    return store

                half = 0.5 * step_size
                advance(
                    [
                        (OWN, up, down, p, n, OWN, half, keep(MID + OWN, n)),
                        (
                            NEAR,
                            near_up,
                            near_down,
                            near_q,
                            i,
                            NEAR,
                            half,
                            keep(MID + NEAR, i),
                        ),
                    ]
                )

                @pl.when(n < pairs)
                def _():
                    mid_copy(n).start()


            @pl.when(jnp.logical_and(n >= 0, n < limit))
            def _():
                shift = jnp.where(jnp.logical_or(is_final, is_top), MID, 0)
                source = jnp.where(
                    kind == TOP, FAR, jnp.where(is_near | is_top, NEAR, OWN)
                )
                above = jnp.where(is_near, near_up, up)
                above = jnp.where(kind >= TOP, FAR, above)
                below = jnp.where(is_near, near_down, down)
                below = jnp.where(kind == TOP, NEAR, jnp.where(is_top, OWN, below))
                row = jnp.where(is_near, near_q, p)
                row = jnp.where(kind == TOP, p + 2, jnp.where(is_top, p + 1, row))

                def store(real, imag):
                    @pl.when(is_final)
                    def _():
                        out_ref[0, n, 0] = real
                        out_ref[0, n, 1] = imag

                    @pl.when(jnp.logical_not(is_final))
                    def _():
                        into = MID + jnp.where(is_top, FAR, source)
                        at = jnp.where(is_top, n + 1, n)
                        rho[into, at, 0] = real
                        rho[into, at, 1] = imag

                advance(
                    [
                        (
                            shift + source,
                            shift + above,
                            shift + below,
                            row,
                            n,
                            source,
                            jnp.where(shift > 0, step_size, 0.5 * step_size),
                            store,
                        )
                    ]
                )

                @pl.when(jnp.logical_and(is_own, n < pairs))
                def _():
                    mid_copy(n).start()

                @pl.when(is_top)
                def _():
                    top_copy(n).start()

    @pl.when(p == 2)
    def _():
        for i in range(N - 4, N - 2):
            top_copy(i).wait_recv()

    partner_copy().wait_send()

    aside = jnp.where(p == 4, 2, 0)
    sends = (
        direct_count,
        pairs,
        relay_near_count + aside,
        relay_far_count + aside - jnp.where(p == 1, 2, 0),
    )
    for row, count in enumerate(sends):
        for k in range(1, N + 1):

            @pl.when(count == k)
            def _(row=row, k=k):
                pltpu.make_async_remote_copy(
                    src_ref=rho.at[OWN, 0:k],
                    dst_ref=rho.at[OWN, 0:k],
                    send_sem=send_sem.at[row],
                    recv_sem=recv_sem.at[0, 0],
                    device_id={"na": p + 1 - 2 * core},
                    device_id_type=MESH,
                ).wait_send()


def per_device(hierarchy, hamiltonian, couplings, damp_rates, coef_real, coef_imag):
    total = hierarchy.shape[1]
    M = hierarchy.shape[-1]
    hbm = pl.BlockSpec(memory_space=pltpu.HBM)
    return pl.pallas_call(
        functools.partial(kernel, total, M),
        out_shape=pltpu.VMEM(hierarchy.shape, jnp.float32),
        in_specs=[hbm] * 6,
        out_specs=pl.BlockSpec(memory_space=pltpu.VMEM),
        scratch_shapes=[
            pltpu.VMEM((MID + 4, total, 2, M, M), jnp.float32),
            pltpu.VMEM((2 * M, 6 * M), jnp.bfloat16),
            pltpu.VMEM((6 * M, 2 * M), jnp.bfloat16),
            pltpu.VMEM((6 * M, 4 * M), jnp.bfloat16),
            pltpu.VMEM((4 * M, 6 * M), jnp.bfloat16),
            pltpu.VMEM((6, total, 8, M), jnp.float32),
            pltpu.VMEM((3, M, M), jnp.float32),
            pltpu.SMEM(damp_rates.shape, jnp.float32),
            pltpu.SMEM(coef_real.shape, jnp.float32),
            pltpu.SMEM(coef_imag.shape, jnp.float32),
            pltpu.SemaphoreType.DMA((3,)),
            pltpu.SemaphoreType.DMA((3,)),
            pltpu.SemaphoreType.DMA((3,)),
            pltpu.SemaphoreType.DMA((4,)),
            pltpu.SemaphoreType.DMA((3, total)),
        ],
        compiler_params=pltpu.CompilerParams(
            collective_id=0, has_side_effects=True, vmem_limit_bytes=(8 + total) * 2**20
        ),
    )(
        *(
            pltpu.with_memory_space_constraint(x, pltpu.HBM)
            for x in (
                hierarchy,
                hamiltonian,
                couplings,
                damp_rates,
                coef_real,
                coef_imag,
            )
        )
    )


def solution(mesh):
    in_specs = (
        P(("sweep", "na"), None, None, None, None),
        P(),
        P(),
        P("sweep"),
        P("sweep"),
        P("sweep"),
    )
    out_specs = P(("sweep", "na"), None, None, None, None)
    return jax.shard_map(
        per_device, mesh=mesh, in_specs=in_specs, out_specs=out_specs, check_vma=False
    )
```
